32 devices in a mesh: outer: 8 (over z, core), inner: 4 (over y, x).
Axes of the slice: x: 2, y: 2, z: 4, core: 2. Of those that a mesh axis runs over, the one named last changes fastest.
Arguments:
- leaf_blocks: float32 [32, 512, 512], P(('outer', 'inner')), as said below
- leaf_bases: float32 [32, 512, 256], P(('outer', 'inner'))
- local_gens: float32 [32, 2, 256, 256], P(('outer', 'inner'))
- chain_gens: float32 [64, 2, 256, 256], P(('outer', 'inner')), as said below
- node_ranks: int32 [3, 32], replicated, may hold values from 192 to 256, as said below
Outputs:
- local_reduced: float32 [32, 256, 256], P(('outer', 'inner'))
- chain_reduced: float32 [64, 256, 256], P(('outer', 'inner'))
- top_factor: float32 [16384, 512], P(('outer', 'inner'))
The draws below stay inside these ranges and needn't reach their ends.
Inputs may be any that keep to these rules, and one draw needn't show every extreme that they name: `node_ranks`: ranks of all tree levels, entry [v, k] read for k < 32 >> v; both ends of the range occur in every draw. `leaf_blocks`: each leaf block is symmetric positive definite. Rows of chain_gens that belong to the same node are equal on all devices below that node.
All inputs are finite; a program needn't handle non-finite values.
Results may differ from the reference program's by a relative error of at most 0.00017.
Values sent between devices are 32-bit elements; how exact they have to be, the bound alone decides.
A program may use at most 128 MiB of HBM per device.

```python
import math
import jax
import jax.numpy as jnp
from jax import lax

RANK = 256
LEAF = 512
LEAF_DEV = 1
LOCAL_LEVELS = 0
IN_LEVELS = 2
LEVELS = 3
LOCAL_NODES = 1
LEAVES = 32
DEVICES = 32


def random_noise(key, shape):
    return jax.random.normal(key, shape, jnp.float32)


def node_gens(key, level_id, node_id):
    node_key = jax.random.fold_in(jax.random.fold_in(key, level_id + 101), node_id)
    key_transfer, key_diagonal, key_coupling = jax.random.split(node_key, 3)
    row_ids = jnp.arange(RANK, dtype=jnp.int32)[:, None]
    col_ids = jnp.arange(RANK, dtype=jnp.int32)[None, :]
    is_odd = node_id % 2 == 1
    target = jnp.where(is_odd, 2 * col_ids - RANK, 2 * col_ids)
    in_half = jnp.where(is_odd, col_ids >= RANK // 2, col_ids < RANK // 2)
    dominant = ((row_ids == target) & in_half).astype(jnp.float32)
    transfer = dominant + random_noise(key_transfer, (RANK, RANK)) * (0.25 / math.sqrt(2 * RANK))
    diagonal = jax.random.uniform(key_diagonal, (RANK,), jnp.float32, -0.25, 0.25)
    coupling = jnp.diag(diagonal) + random_noise(key_coupling, (RANK, RANK)) * (0.06 / math.sqrt(RANK))
    return jnp.stack([transfer, coupling])


def draw_leaf_blocks(key, part):
    key_diagonal, key_noise = jax.random.split(jax.random.fold_in(key, 11))
    diagonal = jnp.exp(jax.random.uniform(key_diagonal, (LEAVES, LEAF), jnp.float32, math.log(3.0), math.log(8.0)))
    random_part = random_noise(key_noise, (LEAVES, LEAF, LEAF))
    symmetric = (random_part + jnp.swapaxes(random_part, 1, 2)) * (1.0 / math.sqrt(2.0 * LEAF))
    return symmetric + diagonal[:, :, None] * jnp.eye(LEAF, dtype=jnp.float32)[None, :, :]


def draw_leaf_bases(key, part):
    key_noise = jax.random.fold_in(key, 12)
    row_ids = jnp.arange(LEAF, dtype=jnp.int32)[:, None]
    col_ids = jnp.arange(RANK, dtype=jnp.int32)[None, :]
    dominant = (row_ids == 2 * col_ids).astype(jnp.float32)
    return dominant[None, :, :] + random_noise(key_noise, (LEAVES, LEAF, RANK)) * (0.25 / math.sqrt(LEAF))


def draw_local_gens(key, part):
    levels, positions, counts = ([], [], [])
    for tree_level in range(LOCAL_LEVELS + 1):
        per_device = LEAF_DEV >> tree_level
        for position in range(per_device):
            levels.append(tree_level)
            positions.append(position)
            counts.append(per_device)
    device = jnp.arange(DEVICES, dtype=jnp.int32)[:, None]
    level_ids = jnp.broadcast_to(jnp.array(levels, jnp.int32)[None, :], (DEVICES, LOCAL_NODES))
    node_ids = device * jnp.array(counts, jnp.int32)[None, :] + jnp.array(positions, jnp.int32)[None, :]
    gen_key = jax.random.fold_in(key, 13)
    return jax.vmap(lambda level_id, node_id: node_gens(gen_key, level_id, node_id))(level_ids.reshape(-1), node_ids.reshape(-1))


def draw_chain_gens(key, part):
    device = jnp.arange(DEVICES, dtype=jnp.int32)[:, None]
    depths = jnp.arange(1, IN_LEVELS + 1, dtype=jnp.int32)[None, :]
    level_ids = jnp.broadcast_to(LOCAL_LEVELS + depths, (DEVICES, IN_LEVELS))
    node_ids = jnp.right_shift(device, depths)
    gen_key = jax.random.fold_in(key, 13)
    return jax.vmap(lambda level_id, node_id: node_gens(gen_key, level_id, node_id))(level_ids.reshape(-1), node_ids.reshape(-1))


def draw_node_ranks(key, part):
    ranks = jax.random.randint(jax.random.fold_in(key, 14), (LEVELS, LEAVES), 3 * RANK // 4, RANK + 1, jnp.int32)
    return ranks.at[0, 0].set(RANK).at[0, 1].set(3 * RANK // 4)


def setup_inputs(seed: int = 0) -> dict:
    keys = jax.random.split(jax.random.key(seed), 6)
    return {
        "leaf_blocks": draw_leaf_blocks(jax.random.fold_in(keys[5], 71), 0),
        "leaf_bases": draw_leaf_bases(jax.random.fold_in(keys[5], 71), 0),
        "local_gens": draw_local_gens(jax.random.fold_in(keys[5], 71), 0),
        "chain_gens": draw_chain_gens(jax.random.fold_in(keys[5], 71), 0),
        "node_ranks": draw_node_ranks(jax.random.fold_in(keys[5], 71), 0),
    }


PRECISE = lax.Precision.HIGHEST

def column_mask(ranks, rank_width):
    return (jnp.arange(rank_width, dtype=jnp.int32)[None, :] < ranks[:, None]).astype(jnp.float32)

def reduce_node(node_block, node_basis, col_mask):
    factor = jnp.linalg.cholesky(node_block)
    whitened = lax.linalg.triangular_solve(factor, node_basis, left_side=True, lower=True)
    gram_matrix = jnp.dot(whitened.T, whitened, precision=PRECISE) + jnp.diag(1.0 - col_mask)
    gram_factor = jnp.linalg.cholesky(gram_matrix)
    identity = jnp.eye(col_mask.shape[0], dtype=jnp.float32)
    inverse_factor = lax.linalg.triangular_solve(gram_factor, identity, left_side=True, lower=True)
    reduced = jnp.dot(inverse_factor.T, inverse_factor, precision=PRECISE)
    return reduced * col_mask[:, None] * col_mask[None, :]

def assemble(reduced_left, reduced_right, couple_left, couple_right, mask_left, mask_right):
    coupling = (couple_left + couple_right.T) * mask_left[:, None] * mask_right[None, :]
    upper_half = jnp.concatenate([reduced_left, coupling], axis=1)
    lower_half = jnp.concatenate([coupling.T, reduced_right], axis=1)
    row_mask = jnp.concatenate([mask_left, mask_right])
    node_block = jnp.concatenate([upper_half, lower_half], axis=0) + jnp.diag(1.0 - row_mask)
    return (node_block, row_mask)

def merge_pair(reduced_left, reduced_right, gens_left, gens_right, mask_left, mask_right, mask_parent):
    node_block, row_mask = assemble(reduced_left, reduced_right, gens_left[1], gens_right[1], mask_left, mask_right)
    node_basis = jnp.concatenate([gens_left[0], gens_right[0]], axis=0) * row_mask[:, None] * mask_parent[None, :]
    return reduce_node(node_block, node_basis, mask_parent)

def reference(leaf_blocks, leaf_bases, local_gens, chain_gens, node_ranks):
    rank_width = RANK
    local_all = local_gens.reshape(DEVICES, 2 * LEAF_DEV - 1, 2, rank_width, rank_width)
    chain_all = chain_gens.reshape(DEVICES, IN_LEVELS, 2, rank_width, rank_width)
    col_mask = column_mask(node_ranks[0], rank_width)
    reduced = lax.map(lambda element: reduce_node(element[0], element[1] * element[2][None, :], element[2]), (leaf_blocks, leaf_bases, col_mask))
    local_parts = [reduced.reshape(DEVICES, LEAF_DEV, rank_width, rank_width)]
    chain_parts = []
    offset = 0
    top_blocks = None
    for tree_level in range(LOCAL_LEVELS + IN_LEVELS + 1):
        node_count = LEAVES >> tree_level
        if tree_level <= LOCAL_LEVELS:
            per_device = LEAF_DEV >> tree_level
            generators = local_all[:, offset:offset + per_device].reshape(node_count, 2, rank_width, rank_width)
            offset = offset + per_device
        else:
            group_depth = tree_level - LOCAL_LEVELS
            generators = chain_all[::2 ** group_depth, group_depth - 1]
        col_mask = column_mask(node_ranks[tree_level, :node_count], rank_width)
        pair_args = (reduced[0::2], reduced[1::2], generators[0::2], generators[1::2], col_mask[0::2], col_mask[1::2])
        if tree_level == LOCAL_LEVELS + IN_LEVELS:
            top_blocks = lax.map(lambda element: jnp.linalg.cholesky(assemble(element[0], element[1], element[2][1], element[3][1], element[4], element[5])[0]), pair_args)
        else:
            parent_mask = column_mask(node_ranks[tree_level + 1, :node_count // 2], rank_width)
            reduced = lax.map(lambda element: merge_pair(*element), pair_args + (parent_mask,))
            if tree_level + 1 <= LOCAL_LEVELS:
                local_parts.append(reduced.reshape(DEVICES, LEAF_DEV >> tree_level + 1, rank_width, rank_width))
            else:
                chain_parts.append(jnp.repeat(reduced, 2 ** (tree_level + 1 - LOCAL_LEVELS), axis=0))
    local_reduced = jnp.concatenate(local_parts, axis=1).reshape(DEVICES * (2 * LEAF_DEV - 1), rank_width, rank_width)
    chain_reduced = jnp.stack(chain_parts, axis=1).reshape(DEVICES * IN_LEVELS, rank_width, rank_width)
    top_factor = jnp.repeat(top_blocks, 2 ** (IN_LEVELS + 1), axis=0).reshape(DEVICES * 2 * rank_width, 2 * rank_width)
    return (local_reduced, chain_reduced, top_factor)
```

```python
import functools

import jax
import jax.numpy as jnp
from jax import lax
from jax.experimental import pallas as pl
from jax.experimental.pallas import tpu as pltpu
from jax.sharding import PartitionSpec as P

LANES = 128
SUB = 8
PANEL = 32
TOLERANCE = 4e-6
MOST = 40
HIGH = lax.Precision.HIGHEST


def dot(a, b, dims=((1,), (0,))):
    return lax.dot_general(a, b, (dims, ((), ())), precision=HIGH, preferred_element_type=jnp.float32)


NT = ((1,), (1,))
TN = ((0,), (0,))


def thirds(x):
    a = x.astype(jnp.bfloat16)
    x = x - a.astype(jnp.float32)
    b = x.astype(jnp.bfloat16)
    return a, b, (x - b.astype(jnp.float32)).astype(jnp.bfloat16)


def bdot(a, b):
    return jnp.dot(a, b, preferred_element_type=jnp.float32)


def iota(shape, axis):
    return lax.broadcasted_iota(jnp.int32, shape, axis)


def total(terms):
    while len(terms) > 1:
        terms = [a + b for a, b in zip(terms[::2], terms[1::2])]
    return terms[0]


def row_of(x, j):
    return jnp.broadcast_to(x[j : j + 1, :], x.shape)


def col_of(x, c):
    return jnp.broadcast_to(x[:, c : c + 1], x.shape)


def tile_pass(a_ref, keep_ref, reverse, h):
    n = a_ref.shape[0]
    tiles = n // LANES
    groups = PANEL // SUB
    sub = iota((SUB, LANES), 0)
    lane = iota((SUB, LANES), 1)
    wide = iota((n, LANES), 1)

    def order(count):
        return range(count - 1, -1, -1) if reverse else range(count)

    own_at = pl.multiple_of(h * LANES, LANES)
    spots = [own_at] + [pl.multiple_of(lax.rem(h + t, tiles) * LANES, LANES) for t in range(1, tiles)]
    ahead = None
    panels = list(order(LANES // PANEL))
    for q in panels:
        base_row = pl.multiple_of(h * LANES + q * PANEL, PANEL)
        rows = [
            [a_ref[pl.ds(pl.multiple_of(base_row + g * SUB, SUB), SUB), pl.ds(spot, LANES)] for spot in spots]
            for g in range(groups)
        ] if ahead is None else ahead
        for s in order(groups):
            c0 = q * PANEL + s * SUB
            cols = [col_of(rows[s][0], c0 + j) for j in range(SUB)]
            other = {g: [col_of(rows[g][0], c0 + j) for j in range(SUB)] for g in range(groups) if g != s}
            piv = list(rows[s])
            kept = [jnp.zeros((SUB, LANES), jnp.float32) for _ in spots]
            left = list(order(SUB))
            inv = 1.0 / row_of(cols[left[0]], left[0])
            yield
            while left:
                j = left.pop(0)
                here = lane == c0 + j
                at = sub == j
                lines = [row_of(x, j) for x in piv]
                if keep_ref is not None:
                    root = lax.rsqrt(row_of(cols[j], j))
                    kept = [jnp.where(at, x * root, k) for x, k in zip(lines, kept)]
                mult = jnp.where(at, -1.0, cols[j])
                now = inv
                if left:
                    i = left[0]
                    cross = row_of(cols[i], j)
                    inv = 1.0 / (row_of(cols[i], i) - (cross * now) * row_of(cols[j], i))
                lines = [jnp.where(here, 1.0, lines[0])] + lines[1:]
                bases = [jnp.where(at | here, 0.0, piv[0])] + [jnp.where(at, 0.0, x) for x in piv[1:]]
                piv = [y - mult * (x * now) for x, y in zip(lines, bases)]
                for i in left:
                    cols[i] = jnp.where(at, 0.0, cols[i]) - mult * (row_of(cols[i], j) * now)
                yield
            rows[s] = piv
            if keep_ref is not None:
                for spot, k in zip(spots, kept):
                    keep_ref[pl.ds(pl.multiple_of(base_row + s * SUB, SUB), SUB), pl.ds(spot, LANES)] = k
            spread = [[row_of(x, j) for j in range(SUB)] for x in piv]
            inside = (lane >= c0) & (lane < c0 + SUB)
            for g, mult in other.items():
                new = list(rows[g])
                new[0] = jnp.where(inside, 0.0, new[0])
                rows[g] = [x - total([mult[j] * y[j] for j in range(SUB)]) for x, y in zip(new, spread)]
                yield
        weights = []
        for t in range(tiles):
            r1, r2, r3 = thirds(jnp.concatenate([rows[g][t] for g in range(groups)], axis=0))
            blank = jnp.zeros((LANES - 2 * PANEL, LANES), jnp.bfloat16)
            weights.append(jnp.concatenate([r1, r1, r2, r2, r1, r3, blank], axis=0))
        yield

        def updated(at, count):
            inside = (wide[:count] >= q * PANEL) & (wide[:count] < (q + 1) * PANEL)
            own = a_ref[pl.ds(at, count), pl.ds(own_at, LANES)]
            olds = [jnp.where(inside, 0.0, own)] + [a_ref[pl.ds(at, count), pl.ds(spot, LANES)] for spot in spots[1:]]
            x = jnp.where(inside, own, 0.0)
            x = x + pltpu.roll(x, PANEL, 1)
            x = x + pltpu.roll(x, 2 * PANEL, 1)
            l1 = x.astype(jnp.bfloat16).astype(jnp.float32)
            l2 = (x - l1).astype(jnp.bfloat16).astype(jnp.float32)
            l3 = x - l1 - l2
            at_quarter = wide[:count] // PANEL
            one = jnp.where((at_quarter & 1) == 0, l1, l2)
            two = jnp.where(at_quarter == 0, l3, jnp.where(at_quarter == 1, l1, 0.0))
            lhs = jnp.concatenate([one.astype(jnp.bfloat16), two.astype(jnp.bfloat16)], axis=1)
            return [old - bdot(lhs, w) for old, w in zip(olds, weights)]

        ahead = None
        if q != panels[-1]:
            onward = -PANEL if reverse else PANEL
            block = updated(pl.multiple_of(base_row + onward, PANEL), PANEL)
            ahead = [[x[g * SUB : (g + 1) * SUB] for x in block] for g in range(groups)]
        yield
        for spot, x in zip(spots, updated(0, n)):
            a_ref[:, pl.ds(spot, LANES)] = x
        for g in range(groups):
            for spot, x in zip(spots, rows[g]):
                a_ref[pl.ds(pl.multiple_of(base_row + g * SUB, SUB), SUB), pl.ds(spot, LANES)] = x
        yield


def together(passes):
    while passes:
        passes = [p for p in passes if next(p, passes) is not passes]


def eliminate(refs, keeps=None, reverse=False):
    tiles = refs[0].shape[0] // LANES
    keeps = keeps or [None] * len(refs)

    def step(i, carry):
        h = tiles - 1 - i if reverse else i
        together([tile_pass(a, k, reverse, h) for a, k in zip(refs, keeps)])
        return carry

    lax.fori_loop(0, tiles, step, 0)


def unit_rest(n, rank):
    return jnp.where((iota((n, n), 0) == iota((n, n), 1)) & (iota((n, n), 0) >= rank), 1.0, 0.0)


def both(n, rank_row, rank_col, x):
    return jnp.where((iota((n, n), 0) < rank_row) & (iota((n, n), 1) < rank_col), x, 0.0)


def place():
    return lax.axis_index("outer") * lax.axis_size("inner") + lax.axis_index("inner")


def rank_at(rank_ref, depth, flip=0, up=0):
    return rank_ref[depth + up, jnp.bitwise_xor(jnp.right_shift(place(), depth + up), flip)]


def product(a, b, nt=False):
    return lax.dot_general(a, b, (NT if nt else ((1,), (0,)), ((), ())), preferred_element_type=jnp.float32)


def dot6(a, b, nt=False):
    (a1, a2, a3), (b1, b2, b3) = a, b
    axis = 1 if nt else 0
    small = product(jnp.concatenate([a2, a1, a3], axis=1), jnp.concatenate([b2, b3, b1], axis=axis), nt)
    large = product(jnp.concatenate([a2, a1, a1], axis=1), jnp.concatenate([b1, b2, b1], axis=axis), nt)
    return small + large


def dot3(a, b, nt=False):
    axis = 1 if nt else 0
    small = product(jnp.concatenate([a[1], a[0]], axis=1), jnp.concatenate([b[0], b[1]], axis=axis), nt)
    return small + product(a[0], b[0], nt)


def slow_dot(out_ref, a_ref, b_ref, dims=((1,), (0,)), add=False):
    n = out_ref.shape[0]

    def rows(i, carry):
        at = pl.ds(pl.multiple_of(i * PANEL, PANEL), PANEL)
        x = dot(a_ref[at, :], b_ref[...], dims)
        out_ref[at, :] = x + b_ref[at, :] if add else x
        return carry

    lax.fori_loop(0, n // PANEL, rows, 0)


def square_sum(x):
    return jnp.sum(x * x)


def neumann(steps, x_ref, y_ref, s_ref, z, hold_ref, work):
    z_ref, p_ref, q_ref, w_ref = work
    s = thirds(s_ref[...])
    a = dot3(thirds(x_ref[...]), s)
    u = dot3(s, thirds(y_ref[...]))
    power = thirds(dot3(thirds(a), thirds(u), nt=True))
    hold_ref[...] = z
    z = z + dot3(power, thirds(z))
    for _ in range(steps - 1):
        raised = dot3(power, power)
        power = thirds(raised)
        z = z + dot3(power, thirds(z))
    z_ref[...] = z

    @pl.when(square_sum(raised) > TOLERANCE)
    def _():
        slow_dot(p_ref, x_ref, s_ref)
        slow_dot(q_ref, s_ref, y_ref)
        slow_dot(w_ref, p_ref, q_ref, NT)
        z_ref[...] = hold_ref[...]

        def more(carry):
            count, rest = carry
            return (count < MOST) & (rest > TOLERANCE)

        def raise_power(carry):
            count, _ = carry
            slow_dot(p_ref, w_ref, z_ref, add=True)
            z_ref[...] = p_ref[...]
            slow_dot(q_ref, w_ref, w_ref)
            rest = square_sum(w_ref[...])
            w_ref[...] = q_ref[...]
            return count + 1, rest

        lax.while_loop(more, raise_power, (jnp.int32(0), jnp.float32(1.0)))


def combine(steps, x_ref, y_ref, s_ref, px, py, g_ref, work):
    py3 = thirds(py)
    t = thirds(dot6(thirds(y_ref[...]), py3))
    y = px - dot6(thirds(s_ref[...]), t)
    z = dot6(thirds(x_ref[...]), thirds(y))
    g = dot6(thirds(py.T), t)
    turned = y.T
    neumann(steps, x_ref, y_ref, s_ref, z, g_ref, work)
    return g + dot6(thirds(turned), thirds(work[0][...]))


def leaf_kernel(rank_ref, m_ref, v_ref, g_ref, x_ref, y_ref, s_ref, *work):
    n = g_ref.shape[0]
    rank = rank_ref[0, place()]
    keep = iota((n, n), 1) < rank
    x_ref[...] = m_ref[:n, :n]
    y_ref[...] = m_ref[n:, n:]
    s_ref[...] = m_ref[:n, n:]
    eliminate([x_ref, y_ref])
    px = jnp.where(keep, v_ref[:n, :], 0.0)
    py = jnp.where(keep, v_ref[n:, :], 0.0)
    g_ref[...] = combine(3, x_ref, y_ref, s_ref, px, py, g_ref, work) + unit_rest(n, rank)


def merge_kernel(depth, rank_ref, x_ref, y_ref, mine_ref, theirs_ref, g_ref, s_ref, *work):
    n = g_ref.shape[0]
    rx, ry, rp = rank_at(rank_ref, depth), rank_at(rank_ref, depth, 1), rank_at(rank_ref, depth, 0, 1)
    s_ref[...] = both(n, rx, ry, mine_ref[1] + theirs_ref[1].T)
    px = both(n, rx, rp, mine_ref[0])
    py = both(n, ry, rp, theirs_ref[0])
    g_ref[...] = combine(2, x_ref, y_ref, s_ref, px, py, g_ref, work) + unit_rest(n, rp)


def first_kernel(g_ref, half_ref):
    half_ref[...] = g_ref[...]
    together([tile_pass(half_ref, None, False, 0)])


def middle_kernel(depth, rank_ref, before_ref, g_ref, l_ref, half_ref, a_ref):
    n = g_ref.shape[0]
    a_ref[...] = before_ref[...]
    half_ref[...] = g_ref[...]
    together([tile_pass(a_ref, None, False, 1), tile_pass(half_ref, None, False, 0)])
    rank = rank_at(rank_ref, depth - 1)
    l_ref[...] = both(n, rank, rank, a_ref[...])


def final_kernel(depth, rank_ref, before_ref, l_ref, a_ref):
    n = l_ref.shape[0]
    a_ref[...] = before_ref[...]
    together([tile_pass(a_ref, None, False, 1)])
    rank = rank_at(rank_ref, depth - 1)
    l_ref[...] = both(n, rank, rank, a_ref[...])


def factor_of(n, e):
    row, col = iota((n, n), 0), iota((n, n), 1)
    upper = jnp.where(row < col, e, 0.0) + jnp.where(row == col, 1.0 / jnp.where(row == col, e, 1.0), 0.0)
    return upper.T


def top_kernel(depth, rank_ref, g_ref, go_ref, c_ref, co_ref, f_ref, l_ref, a_ref, b_ref, ka_ref, kb_ref, s_ref, *work):
    n = g_ref.shape[0]
    pos = lax.axis_index("outer")
    first = jnp.bitwise_and(pos, 1) == 0
    node = jnp.bitwise_and(pos, -2)
    ra, rb = rank_ref[depth, node], rank_ref[depth, node + 1]
    row, col = iota((n, n), 0), iota((n, n), 1)
    pick = jnp.where(first, 1, 0) + jnp.zeros((n, n), jnp.int32) > 0
    a_ref[...] = jnp.where(pick, g_ref[...], go_ref[...])
    b_ref[...] = jnp.where(pick, go_ref[...], g_ref[...])
    ca = jnp.where(pick, c_ref[...], co_ref[...])
    cb = jnp.where(pick, co_ref[...], c_ref[...])
    s_ref[...] = both(n, rb, ra, ca.T + cb)
    neumann(2, b_ref, a_ref, s_ref, b_ref[...], l_ref, work)
    b_ref[...] = work[0][...]
    back = dot6(thirds(dot6(thirds(s_ref[...]), thirds(a_ref[...]))), thirds(s_ref[...]), nt=True)
    l_ref[...] = back
    eliminate([a_ref, b_ref], [ka_ref, kb_ref], reverse=True)
    e = ka_ref[...]
    rank = jnp.where(first, ra, rb)
    l_ref[...] = both(n, rank, rank, jnp.where(pick, a_ref[...], b_ref[...] + l_ref[...]))
    f_ref[:n, :n] = factor_of(n, e)
    f_ref[:n, n:] = jnp.zeros((n, n), jnp.float32)
    f_ref[n:, :n] = dot6(thirds(s_ref[...]), thirds(jnp.where(row >= col, e, 0.0)), nt=True)
    f_ref[n:, n:] = factor_of(n, kb_ref[...])


def call(kernel, name, outs, n, scratch, *arrays, ranks=None, flops=10**9):
    vmem = pl.BlockSpec(memory_space=pltpu.VMEM)
    lead = [] if ranks is None else [pl.BlockSpec(memory_space=pltpu.SMEM)]
    return pl.pallas_call(
        kernel,
        name=name,
        out_shape=[jax.ShapeDtypeStruct(shape, jnp.float32) for shape in outs],
        in_specs=lead + [vmem] * len(arrays),
        out_specs=[vmem] * len(outs),
        scratch_shapes=[pltpu.VMEM((n, n), jnp.float32)] * scratch,
        cost_estimate=pl.CostEstimate(flops=flops, bytes_accessed=4 * 10**6, transcendentals=0),
    )(*([] if ranks is None else [ranks]), *arrays)


def partner(x, axis, bit):
    return lax.ppermute(x, axis, [(i, i ^ 1 << bit) for i in range(lax.axis_size(axis))])


def body(leaf_blocks, leaf_bases, local_gens, chain_gens, node_ranks):
    n = leaf_bases.shape[2]
    in_levels = chain_gens.shape[0]
    square = (n, n)
    gens = [local_gens[0]] + [chain_gens[d] for d in range(in_levels)]
    others = [partner(gens[d], "inner", d) for d in range(in_levels)]
    couple = gens[in_levels][1]
    other_couple = partner(couple, "outer", 0)
    g = call(leaf_kernel, "leaf", [square], n, 7, leaf_blocks[0], leaf_bases[0], ranks=node_ranks, flops=8 * 10**9)[0]
    reduced = []
    half = None
    for depth in range(in_levels):
        g_other = partner(g, "inner", depth)
        if depth == 0:
            half = call(first_kernel, "first", [square], n, 0, g, flops=4 * 10**9)[0]
        else:
            middle = functools.partial(middle_kernel, depth)
            done, half = call(middle, "middle", [square] * 2, n, 1, half, g, ranks=node_ranks, flops=4 * 10**9)
            reduced.append(done)
        merge = functools.partial(merge_kernel, depth)
        g = call(merge, "merge", [square], n, 5, g, g_other, gens[depth], others[depth], ranks=node_ranks)[0]
    g_other = partner(g, "outer", 0)
    final = functools.partial(final_kernel, in_levels)
    reduced.append(call(final, "final", [square], n, 1, half, ranks=node_ranks, flops=4 * 10**9)[0])
    top = functools.partial(top_kernel, in_levels)
    arrays = (g, g_other, couple, other_couple)
    factor, done = call(top, "top", [(2 * n, 2 * n), square], n, 9, *arrays, ranks=node_ranks, flops=4 * 10**9)
    reduced.append(done)
    return (reduced[0][None], jnp.stack(reduced[1:], axis=0), factor)


def solution(mesh):
    return jax.shard_map(
        body,
        mesh=mesh,
        in_specs=(
            P(("outer", "inner"), None, None),
            P(("outer", "inner"), None, None),
            P(("outer", "inner"), None, None, None),
            P(("outer", "inner"), None, None, None),
            P(),
        ),
        out_specs=(
            P(("outer", "inner"), None, None),
            P(("outer", "inner"), None, None),
            P(("outer", "inner"), None),
        ),
        check_vma=False,
    )
```

```python
import functools

import jax
import jax.numpy as jnp
from jax import lax
from jax.experimental import pallas as pl
from jax.experimental.pallas import tpu as pltpu
from jax.sharding import PartitionSpec as P

LANES = 128
SUB = 8
PANEL = 32
TOLERANCE = 4e-6
MOST = 40
GRANT = 20 * 2**20
HIGH = lax.Precision.HIGHEST


def dot(a, b, dims=((1,), (0,))):
    return lax.dot_general(a, b, (dims, ((), ())), precision=HIGH, preferred_element_type=jnp.float32)


NT = ((1,), (1,))


def thirds(x):
    a = x.astype(jnp.bfloat16)
    x = x - a.astype(jnp.float32)
    b = x.astype(jnp.bfloat16)
    return a, b, (x - b.astype(jnp.float32)).astype(jnp.bfloat16)


def bdot(a, b):
    return jnp.dot(a, b, preferred_element_type=jnp.float32)


def iota(shape, axis):
    return lax.broadcasted_iota(jnp.int32, shape, axis)


def total(terms):
    while len(terms) > 1:
        terms = [a + b for a, b in zip(terms[::2], terms[1::2])]
    return terms[0]


def row_of(x, j):
    return jnp.broadcast_to(x[j : j + 1, :], x.shape)


def col_of(x, c):
    return jnp.broadcast_to(x[:, c : c + 1], x.shape)


def tile_pass(a_ref, keep_ref, reverse, h):
    n = a_ref.shape[0]
    tiles = n // LANES
    groups = PANEL // SUB
    sub = iota((SUB, LANES), 0)
    lane = iota((SUB, LANES), 1)
    wide = iota((n, LANES), 1)

    def order(count):
        return range(count - 1, -1, -1) if reverse else range(count)

    own_at = pl.multiple_of(h * LANES, LANES)
    spots = [own_at] + [pl.multiple_of(lax.rem(h + t, tiles) * LANES, LANES) for t in range(1, tiles)]
    ahead = None
    panels = list(order(LANES // PANEL))
    for q in panels:
        base_row = pl.multiple_of(h * LANES + q * PANEL, PANEL)
        rows = [
            [a_ref[pl.ds(pl.multiple_of(base_row + g * SUB, SUB), SUB), pl.ds(spot, LANES)] for spot in spots]
            for g in range(groups)
        ] if ahead is None else ahead
        for s in order(groups):
            c0 = q * PANEL + s * SUB
            cols = [col_of(rows[s][0], c0 + j) for j in range(SUB)]
            other = {g: [col_of(rows[g][0], c0 + j) for j in range(SUB)] for g in range(groups) if g != s}
            piv = list(rows[s])
            kept = [jnp.zeros((SUB, LANES), jnp.float32) for _ in spots]
            left = list(order(SUB))
            inv = 1.0 / row_of(cols[left[0]], left[0])
            yield
            while left:
                j = left.pop(0)
                here = lane == c0 + j
                at = sub == j
                lines = [row_of(x, j) for x in piv]
                if keep_ref is not None:
                    root = lax.rsqrt(row_of(cols[j], j))
                    kept = [jnp.where(at, x * root, k) for x, k in zip(lines, kept)]
                mult = jnp.where(at, -1.0, cols[j])
                now = inv
                if left:
                    i = left[0]
                    cross = row_of(cols[i], j)
                    inv = 1.0 / (row_of(cols[i], i) - (cross * now) * row_of(cols[j], i))
                lines = [jnp.where(here, 1.0, lines[0])] + lines[1:]
                bases = [jnp.where(at | here, 0.0, piv[0])] + [jnp.where(at, 0.0, x) for x in piv[1:]]
                piv = [y - mult * (x * now) for x, y in zip(lines, bases)]
                for i in left:
                    cols[i] = jnp.where(at, 0.0, cols[i]) - mult * (row_of(cols[i], j) * now)
                yield
            rows[s] = piv
            if keep_ref is not None:
                for spot, k in zip(spots, kept):
                    keep_ref[pl.ds(pl.multiple_of(base_row + s * SUB, SUB), SUB), pl.ds(spot, LANES)] = k
            spread = [[row_of(x, j) for j in range(SUB)] for x in piv]
            inside = (lane >= c0) & (lane < c0 + SUB)
            for g, mult in other.items():
                new = list(rows[g])
                new[0] = jnp.where(inside, 0.0, new[0])
                rows[g] = [x - total([mult[j] * y[j] for j in range(SUB)]) for x, y in zip(new, spread)]
                yield
        weights = []
        for t in range(tiles):
            r1, r2, r3 = thirds(jnp.concatenate([rows[g][t] for g in range(groups)], axis=0))
            blank = jnp.zeros((LANES - 2 * PANEL, LANES), jnp.bfloat16)
            weights.append(jnp.concatenate([r1, r1, r2, r2, r1, r3, blank], axis=0))
        yield

        def updated(at, count):
            inside = (wide[:count] >= q * PANEL) & (wide[:count] < (q + 1) * PANEL)
            own = a_ref[pl.ds(at, count), pl.ds(own_at, LANES)]
            olds = [jnp.where(inside, 0.0, own)] + [a_ref[pl.ds(at, count), pl.ds(spot, LANES)] for spot in spots[1:]]
            x = jnp.where(inside, own, 0.0)
            x = x + pltpu.roll(x, PANEL, 1)
            x = x + pltpu.roll(x, 2 * PANEL, 1)
            l1 = x.astype(jnp.bfloat16).astype(jnp.float32)
            l2 = (x - l1).astype(jnp.bfloat16).astype(jnp.float32)
            l3 = x - l1 - l2
            at_quarter = wide[:count] // PANEL
            one = jnp.where((at_quarter & 1) == 0, l1, l2)
            two = jnp.where(at_quarter == 0, l3, jnp.where(at_quarter == 1, l1, 0.0))
            lhs = jnp.concatenate([one.astype(jnp.bfloat16), two.astype(jnp.bfloat16)], axis=1)
            return [old - bdot(lhs, w) for old, w in zip(olds, weights)]

        ahead = None
        if q != panels[-1]:
            onward = -PANEL if reverse else PANEL
            block = updated(pl.multiple_of(base_row + onward, PANEL), PANEL)
            ahead = [[x[g * SUB : (g + 1) * SUB] for x in block] for g in range(groups)]
        yield
        for spot, x in zip(spots, updated(0, n)):
            a_ref[:, pl.ds(spot, LANES)] = x
        for g in range(groups):
            for spot, x in zip(spots, rows[g]):
                a_ref[pl.ds(pl.multiple_of(base_row + g * SUB, SUB), SUB), pl.ds(spot, LANES)] = x
        yield


def together(passes):
    while passes:
        passes = [p for p in passes if next(p, passes) is not passes]


def eliminate(refs, keeps=None, reverse=False):
    tiles = refs[0].shape[0] // LANES
    keeps = keeps or [None] * len(refs)

    def step(i, carry):
        h = tiles - 1 - i if reverse else i
        together([tile_pass(a, k, reverse, h) for a, k in zip(refs, keeps)])
        return carry

    lax.fori_loop(0, tiles, step, 0)


def unit_rest(n, rank):
    return jnp.where((iota((n, n), 0) == iota((n, n), 1)) & (iota((n, n), 0) >= rank), 1.0, 0.0)


def both(n, rank_row, rank_col, x):
    return jnp.where((iota((n, n), 0) < rank_row) & (iota((n, n), 1) < rank_col), x, 0.0)


def place():
    return lax.axis_index("outer") * lax.axis_size("inner") + lax.axis_index("inner")


def rank_at(rank_ref, depth, flip=0, up=0):
    return rank_ref[depth + up, jnp.bitwise_xor(jnp.right_shift(place(), depth + up), flip)]


def product(a, b, nt=False):
    return lax.dot_general(a, b, (NT if nt else ((1,), (0,)), ((), ())), preferred_element_type=jnp.float32)


def dot6(a, b, nt=False):
    (a1, a2, a3), (b1, b2, b3) = a, b
    axis = 1 if nt else 0
    small = product(jnp.concatenate([a2, a1, a3], axis=1), jnp.concatenate([b2, b3, b1], axis=axis), nt)
    large = product(jnp.concatenate([a2, a1, a1], axis=1), jnp.concatenate([b1, b2, b1], axis=axis), nt)
    return small + large


def dot3(a, b, nt=False):
    axis = 1 if nt else 0
    small = product(jnp.concatenate([a[1], a[0]], axis=1), jnp.concatenate([b[0], b[1]], axis=axis), nt)
    return small + product(a[0], b[0], nt)


def slow_dot(out_ref, a_ref, b_ref, dims=((1,), (0,)), add=False):
    n = out_ref.shape[0]

    def rows(i, carry):
        at = pl.ds(pl.multiple_of(i * PANEL, PANEL), PANEL)
        x = dot(a_ref[at, :], b_ref[...], dims)
        out_ref[at, :] = x + b_ref[at, :] if add else x
        return carry

    lax.fori_loop(0, n // PANEL, rows, 0)


def square_sum(x):
    return jnp.sum(x * x)


def neumann(steps, x_ref, y_ref, s_ref, z, hold_ref, work):
    z_ref, p_ref, q_ref, w_ref = work
    s = thirds(s_ref[...])
    a = dot3(thirds(x_ref[...]), s)
    u = dot3(s, thirds(y_ref[...]))
    power = thirds(dot3(thirds(a), thirds(u), nt=True))
    hold_ref[...] = z
    z = z + dot3(power, thirds(z))
    for _ in range(steps - 1):
        raised = dot3(power, power)
        power = thirds(raised)
        z = z + dot3(power, thirds(z))
    z_ref[...] = z

    @pl.when(square_sum(raised) > TOLERANCE)
    def _():
        slow_dot(p_ref, x_ref, s_ref)
        slow_dot(q_ref, s_ref, y_ref)
        slow_dot(w_ref, p_ref, q_ref, NT)
        z_ref[...] = hold_ref[...]

        def more(carry):
            count, rest = carry
            return (count < MOST) & (rest > TOLERANCE)

        def raise_power(carry):
            count, _ = carry
            slow_dot(p_ref, w_ref, z_ref, add=True)
            z_ref[...] = p_ref[...]
            slow_dot(q_ref, w_ref, w_ref)
            rest = square_sum(w_ref[...])
            w_ref[...] = q_ref[...]
            return count + 1, rest

        lax.while_loop(more, raise_power, (jnp.int32(0), jnp.float32(1.0)))


def combine(steps, x_ref, y_ref, s_ref, px, py, g_ref, work):
    py3 = thirds(py)
    t = thirds(dot6(thirds(y_ref[...]), py3))
    y = px - dot6(thirds(s_ref[...]), t)
    z = dot6(thirds(x_ref[...]), thirds(y))
    g = dot6(thirds(py.T), t)
    turned = y.T
    neumann(steps, x_ref, y_ref, s_ref, z, g_ref, work)
    return g + dot6(thirds(turned), thirds(work[0][...]))


def leaf_kernel(rank_ref, m_ref, v_ref, g_ref, x_ref, y_ref, s_ref, *work):
    n = g_ref.shape[0]
    rank = rank_ref[0, place()]
    keep = iota((n, n), 1) < rank
    x_ref[...] = m_ref[:n, :n]
    y_ref[...] = m_ref[n:, n:]
    s_ref[...] = m_ref[:n, n:]
    eliminate([x_ref, y_ref])
    px = jnp.where(keep, v_ref[:n, :], 0.0)
    py = jnp.where(keep, v_ref[n:, :], 0.0)
    g_ref[...] = combine(3, x_ref, y_ref, s_ref, px, py, g_ref, work) + unit_rest(n, rank)


def merge_kernel(depth, rank_ref, x_ref, y_ref, mine_ref, theirs_ref, g_ref, s_ref, *work):
    n = g_ref.shape[0]
    rx, ry, rp = rank_at(rank_ref, depth), rank_at(rank_ref, depth, 1), rank_at(rank_ref, depth, 0, 1)
    s_ref[...] = both(n, rx, ry, mine_ref[1] + theirs_ref[1].T)
    px = both(n, rx, rp, mine_ref[0])
    py = both(n, ry, rp, theirs_ref[0])
    g_ref[...] = combine(2, x_ref, y_ref, s_ref, px, py, g_ref, work) + unit_rest(n, rp)


def first_kernel(g_ref, half_ref):
    half_ref[...] = g_ref[...]
    together([tile_pass(half_ref, None, False, 0)])


def middle_kernel(depth, rank_ref, before_ref, g_ref, l_ref, half_ref, a_ref):
    n = g_ref.shape[0]
    a_ref[...] = before_ref[...]
    half_ref[...] = g_ref[...]
    together([tile_pass(a_ref, None, False, 1), tile_pass(half_ref, None, False, 0)])
    rank = rank_at(rank_ref, depth - 1)
    l_ref[...] = both(n, rank, rank, a_ref[...])


def final_kernel(depth, rank_ref, before_ref, l_ref, a_ref):
    n = l_ref.shape[0]
    a_ref[...] = before_ref[...]
    together([tile_pass(a_ref, None, False, 1)])
    rank = rank_at(rank_ref, depth - 1)
    l_ref[...] = both(n, rank, rank, a_ref[...])


def factor_of(n, e):
    row, col = iota((n, n), 0), iota((n, n), 1)
    upper = jnp.where(row < col, e, 0.0) + jnp.where(row == col, 1.0 / jnp.where(row == col, e, 1.0), 0.0)
    return upper.T


def top_kernel(depth, rank_ref, g_ref, go_ref, c_ref, co_ref, *refs):
    n = g_ref.shape[0]
    lower, (f_ref, out_ref, l_ref, a_ref, b_ref, ka_ref, kb_ref, s_ref), work = refs[: depth - 1], refs[depth - 1 : depth + 7], refs[depth + 7 :]
    for i, ref in enumerate(lower):
        out_ref[i] = ref[...]
    pos = lax.axis_index("outer")
    first = jnp.bitwise_and(pos, 1) == 0
    node = jnp.bitwise_and(pos, -2)
    ra, rb = rank_ref[depth, node], rank_ref[depth, node + 1]
    row, col = iota((n, n), 0), iota((n, n), 1)
    pick = jnp.where(first, 1, 0) + jnp.zeros((n, n), jnp.int32) > 0
    a_ref[...] = jnp.where(pick, g_ref[...], go_ref[...])
    b_ref[...] = jnp.where(pick, go_ref[...], g_ref[...])
    ca = jnp.where(pick, c_ref[...], co_ref[...])
    cb = jnp.where(pick, co_ref[...], c_ref[...])
    s_ref[...] = both(n, rb, ra, ca.T + cb)
    neumann(2, b_ref, a_ref, s_ref, b_ref[...], l_ref, work)
    b_ref[...] = work[0][...]
    back = dot6(thirds(dot6(thirds(s_ref[...]), thirds(a_ref[...]))), thirds(s_ref[...]), nt=True)
    l_ref[...] = back
    eliminate([a_ref, b_ref], [ka_ref, kb_ref], reverse=True)
    e = ka_ref[...]
    rank = jnp.where(first, ra, rb)
    out_ref[depth - 1] = both(n, rank, rank, jnp.where(pick, a_ref[...], b_ref[...] + l_ref[...]))
    f_ref[:n, :n] = factor_of(n, e)
    f_ref[:n, n:] = jnp.zeros((n, n), jnp.float32)
    f_ref[n:, :n] = dot6(thirds(s_ref[...]), thirds(jnp.where(row >= col, e, 0.0)), nt=True)
    f_ref[n:, n:] = factor_of(n, kb_ref[...])


def call(kernel, outs, n, scratch, *arrays, ranks=None, flops=10**9):
    vmem = pl.BlockSpec(memory_space=pltpu.VMEM)
    lead = [] if ranks is None else [pl.BlockSpec(memory_space=pltpu.SMEM)]
    return pl.pallas_call(
        kernel,
        out_shape=[jax.ShapeDtypeStruct(shape, jnp.float32) for shape in outs],
        in_specs=lead + [vmem] * len(arrays),
        out_specs=[vmem] * len(outs),
        scratch_shapes=[pltpu.VMEM((n, n), jnp.float32)] * scratch,
        compiler_params=pltpu.CompilerParams(vmem_limit_bytes=GRANT),
        cost_estimate=pl.CostEstimate(flops=flops, bytes_accessed=4 * 10**6, transcendentals=0),
    )(*([] if ranks is None else [ranks]), *arrays)


def partner(x, axis, bit):
    return lax.ppermute(x, axis, [(i, i ^ 1 << bit) for i in range(lax.axis_size(axis))])


def steps(leaf_blocks, leaf_bases, local_gens, chain_gens, node_ranks):
    n = leaf_bases.shape[2]
    in_levels = chain_gens.shape[0]
    square = (n, n)
    gens = [local_gens[0]] + [chain_gens[d] for d in range(in_levels)]
    others = []
    for d in range(in_levels):
        others.append(partner(gens[d], "inner", d))
    couple = gens[in_levels][1]
    other_couple = partner(couple, "outer", 0)
    g = call(leaf_kernel, [square], n, 7, leaf_blocks[0], leaf_bases[0], ranks=node_ranks, flops=8 * 10**9)[0]
    reduced = []
    half = None
    for depth in range(in_levels):
        g_other = partner(g, "inner", depth)
        if depth == 0:
            half = call(first_kernel, [square], n, 0, g, flops=4 * 10**9)[0]
        else:
            middle = functools.partial(middle_kernel, depth)
            done, half = call(middle, [square] * 2, n, 1, half, g, ranks=node_ranks, flops=4 * 10**9)
            reduced.append(done)
        merge = functools.partial(merge_kernel, depth)
        g = call(merge, [square], n, 5, g, g_other, gens[depth], others[depth], ranks=node_ranks)[0]
    g_other = partner(g, "outer", 0)
    final = functools.partial(final_kernel, in_levels)
    reduced.append(call(final, [square], n, 1, half, ranks=node_ranks, flops=4 * 10**9)[0])
    top = functools.partial(top_kernel, in_levels)
    arrays = (g, g_other, couple, other_couple, *reduced[1:])
    outs = [(2 * n, 2 * n), (in_levels, n, n)]
    factor, chain = call(top, outs, n, 10, *arrays, ranks=node_ranks, flops=4 * 10**9)
    return (reduced[0][None], chain, factor)


def solution(mesh):
    return jax.shard_map(
        steps,
        mesh=mesh,
        in_specs=(
            P(("outer", "inner"), None, None),
            P(("outer", "inner"), None, None),
            P(("outer", "inner"), None, None, None),
            P(("outer", "inner"), None, None, None),
            P(),
        ),
        out_specs=(
            P(("outer", "inner"), None, None),
            P(("outer", "inner"), None, None),
            P(("outer", "inner"), None),
        ),
        check_vma=False,
    )
```

```python
import functools

import jax
import jax.numpy as jnp
from jax import lax
from jax.experimental import pallas as pl
from jax.experimental.pallas import tpu as pltpu
from jax.sharding import PartitionSpec as P

LANES = 128
SUB = 8
PANEL = 32
TOLERANCE = 4e-6
MOST = 40
GRANT = 20 * 2**20
HIGH = lax.Precision.HIGHEST


def dot(a, b, dims=((1,), (0,))):
    return lax.dot_general(a, b, (dims, ((), ())), precision=HIGH, preferred_element_type=jnp.float32)


NT = ((1,), (1,))


def thirds(x):
    a = x.astype(jnp.bfloat16)
    x = x - a.astype(jnp.float32)
    b = x.astype(jnp.bfloat16)
    return a, b, (x - b.astype(jnp.float32)).astype(jnp.bfloat16)


def bdot(a, b):
    return jnp.dot(a, b, preferred_element_type=jnp.float32)


def iota(shape, axis):
    return lax.broadcasted_iota(jnp.int32, shape, axis)


def total(terms):
    while len(terms) > 1:
        terms = [a + b for a, b in zip(terms[::2], terms[1::2])]
    return terms[0]


def row_of(x, j):
    return jnp.broadcast_to(x[j : j + 1, :], x.shape)


def col_of(x, c):
    return jnp.broadcast_to(x[:, c : c + 1], x.shape)


def tile_pass(a_ref, keep_ref, reverse, h):
    n = a_ref.shape[0]
    tiles = n // LANES
    groups = PANEL // SUB
    sub = iota((SUB, LANES), 0)
    lane = iota((SUB, LANES), 1)
    wide = iota((n, LANES), 1)

    def order(count):
        return range(count - 1, -1, -1) if reverse else range(count)

    own_at = pl.multiple_of(h * LANES, LANES)
    spots = [own_at] + [pl.multiple_of(lax.rem(h + t, tiles) * LANES, LANES) for t in range(1, tiles)]
    ahead = None
    panels = list(order(LANES // PANEL))
    for q in panels:
        base_row = pl.multiple_of(h * LANES + q * PANEL, PANEL)
        rows = [
            [a_ref[pl.ds(pl.multiple_of(base_row + g * SUB, SUB), SUB), pl.ds(spot, LANES)] for spot in spots]
            for g in range(groups)
        ] if ahead is None else ahead
        for s in order(groups):
            c0 = q * PANEL + s * SUB
            cols = [col_of(rows[s][0], c0 + j) for j in range(SUB)]
            other = {g: [col_of(rows[g][0], c0 + j) for j in range(SUB)] for g in range(groups) if g != s}
            piv = list(rows[s])
            kept = [jnp.zeros((SUB, LANES), jnp.float32) for _ in spots]
            left = list(order(SUB))
            inv = 1.0 / row_of(cols[left[0]], left[0])
            yield
            while left:
                j = left.pop(0)
                here = lane == c0 + j
                at = sub == j
                lines = [row_of(x, j) for x in piv]
                if keep_ref is not None:
                    root = lax.rsqrt(row_of(cols[j], j))
                    kept = [jnp.where(at, x * root, k) for x, k in zip(lines, kept)]
                mult = jnp.where(at, -1.0, cols[j])
                now = inv
                if left:
                    i = left[0]
                    cross = row_of(cols[i], j)
                    inv = 1.0 / (row_of(cols[i], i) - (cross * now) * row_of(cols[j], i))
                lines = [jnp.where(here, 1.0, lines[0])] + lines[1:]
                bases = [jnp.where(at | here, 0.0, piv[0])] + [jnp.where(at, 0.0, x) for x in piv[1:]]
                piv = [y - mult * (x * now) for x, y in zip(lines, bases)]
                for i in left:
                    cols[i] = jnp.where(at, 0.0, cols[i]) - mult * (row_of(cols[i], j) * now)
                yield
            rows[s] = piv
            if keep_ref is not None:
                for spot, k in zip(spots, kept):
                    keep_ref[pl.ds(pl.multiple_of(base_row + s * SUB, SUB), SUB), pl.ds(spot, LANES)] = k
            spread = [[row_of(x, j) for j in range(SUB)] for x in piv]
            inside = (lane >= c0) & (lane < c0 + SUB)
            for g, mult in other.items():
                new = list(rows[g])
                new[0] = jnp.where(inside, 0.0, new[0])
                rows[g] = [x - total([mult[j] * y[j] for j in range(SUB)]) for x, y in zip(new, spread)]
                yield
        weights = []
        for t in range(tiles):
            r1, r2, r3 = thirds(jnp.concatenate([rows[g][t] for g in range(groups)], axis=0))
            blank = jnp.zeros((LANES - 2 * PANEL, LANES), jnp.bfloat16)
            weights.append(jnp.concatenate([r1, r1, r2, r2, r1, r3, blank], axis=0))
        yield

        def updated(at, count):
            inside = (wide[:count] >= q * PANEL) & (wide[:count] < (q + 1) * PANEL)
            own = a_ref[pl.ds(at, count), pl.ds(own_at, LANES)]
            olds = [jnp.where(inside, 0.0, own)] + [a_ref[pl.ds(at, count), pl.ds(spot, LANES)] for spot in spots[1:]]
            x = jnp.where(inside, own, 0.0)
            x = x + pltpu.roll(x, PANEL, 1)
            x = x + pltpu.roll(x, 2 * PANEL, 1)
            l1 = x.astype(jnp.bfloat16).astype(jnp.float32)
            l2 = (x - l1).astype(jnp.bfloat16).astype(jnp.float32)
            l3 = x - l1 - l2
            at_quarter = wide[:count] // PANEL
            one = jnp.where((at_quarter & 1) == 0, l1, l2)
            two = jnp.where(at_quarter == 0, l3, jnp.where(at_quarter == 1, l1, 0.0))
            lhs = jnp.concatenate([one.astype(jnp.bfloat16), two.astype(jnp.bfloat16)], axis=1)
            return [old - bdot(lhs, w) for old, w in zip(olds, weights)]

        ahead = None
        if q != panels[-1]:
            onward = -PANEL if reverse else PANEL
            block = updated(pl.multiple_of(base_row + onward, PANEL), PANEL)
            ahead = [[x[g * SUB : (g + 1) * SUB] for x in block] for g in range(groups)]
        yield
        for spot, x in zip(spots, updated(0, n)):
            a_ref[:, pl.ds(spot, LANES)] = x
        for g in range(groups):
            for spot, x in zip(spots, rows[g]):
                a_ref[pl.ds(pl.multiple_of(base_row + g * SUB, SUB), SUB), pl.ds(spot, LANES)] = x
        yield


def together(passes):
    while passes:
        passes = [p for p in passes if next(p, passes) is not passes]


def eliminate(refs, keeps=None, reverse=False):
    tiles = refs[0].shape[0] // LANES
    keeps = keeps or [None] * len(refs)

    def step(i, carry):
        h = tiles - 1 - i if reverse else i
        together([tile_pass(a, k, reverse, h) for a, k in zip(refs, keeps)])
        return carry

    lax.fori_loop(0, tiles, step, 0)


def unit_rest(n, rank):
    return jnp.where((iota((n, n), 0) == iota((n, n), 1)) & (iota((n, n), 0) >= rank), 1.0, 0.0)


def both(n, rank_row, rank_col, x):
    return jnp.where((iota((n, n), 0) < rank_row) & (iota((n, n), 1) < rank_col), x, 0.0)


def place():
    return lax.axis_index("outer") * lax.axis_size("inner") + lax.axis_index("inner")


def rank_at(rank_ref, depth, flip=0, up=0):
    return rank_ref[depth + up, jnp.bitwise_xor(jnp.right_shift(place(), depth + up), flip)]


def product(a, b, nt=False):
    return lax.dot_general(a, b, (NT if nt else ((1,), (0,)), ((), ())), preferred_element_type=jnp.float32)


def dot6(a, b, nt=False):
    (a1, a2, a3), (b1, b2, b3) = a, b
    axis = 1 if nt else 0
    small = product(jnp.concatenate([a2, a1, a3], axis=1), jnp.concatenate([b2, b3, b1], axis=axis), nt)
    large = product(jnp.concatenate([a2, a1, a1], axis=1), jnp.concatenate([b1, b2, b1], axis=axis), nt)
    return small + large


def dot3(a, b, nt=False):
    axis = 1 if nt else 0
    small = product(jnp.concatenate([a[1], a[0]], axis=1), jnp.concatenate([b[0], b[1]], axis=axis), nt)
    return small + product(a[0], b[0], nt)


def slow_dot(out_ref, a_ref, b_ref, dims=((1,), (0,)), add=False):
    n = out_ref.shape[0]

    def rows(i, carry):
        at = pl.ds(pl.multiple_of(i * PANEL, PANEL), PANEL)
        x = dot(a_ref[at, :], b_ref[...], dims)
        out_ref[at, :] = x + b_ref[at, :] if add else x
        return carry

    lax.fori_loop(0, n // PANEL, rows, 0)


def square_sum(x):
    return jnp.sum(x * x)


def neumann(steps, x_ref, y_ref, s_ref, z, hold_ref, work):
    z_ref, p_ref, q_ref, w_ref = work
    s = thirds(s_ref[...])
    a = dot3(thirds(x_ref[...]), s)
    u = dot3(s, thirds(y_ref[...]))
    power = thirds(dot3(thirds(a), thirds(u), nt=True))
    hold_ref[...] = z
    z = z + dot3(power, thirds(z))
    for _ in range(steps - 1):
        raised = dot3(power, power)
        power = thirds(raised)
        z = z + dot3(power, thirds(z))
    z_ref[...] = z

    @pl.when(square_sum(raised) > TOLERANCE)
    def _():
        slow_dot(p_ref, x_ref, s_ref)
        slow_dot(q_ref, s_ref, y_ref)
        slow_dot(w_ref, p_ref, q_ref, NT)
        z_ref[...] = hold_ref[...]

        def more(carry):
            count, rest = carry
            return (count < MOST) & (rest > TOLERANCE)

        def raise_power(carry):
            count, _ = carry
            slow_dot(p_ref, w_ref, z_ref, add=True)
            z_ref[...] = p_ref[...]
            slow_dot(q_ref, w_ref, w_ref)
            rest = square_sum(w_ref[...])
            w_ref[...] = q_ref[...]
            return count + 1, rest

        lax.while_loop(more, raise_power, (jnp.int32(0), jnp.float32(1.0)))


def combine(steps, x_ref, y_ref, s_ref, px, py, g_ref, work):
    py3 = thirds(py)
    t = thirds(dot6(thirds(y_ref[...]), py3))
    y = px - dot6(thirds(s_ref[...]), t)
    z = dot6(thirds(x_ref[...]), thirds(y))
    g = dot6(thirds(py.T), t)
    turned = y.T
    neumann(steps, x_ref, y_ref, s_ref, z, g_ref, work)
    return g + dot6(thirds(turned), thirds(work[0][...]))


def leaf_kernel(rank_ref, m_ref, v_ref, g_ref, x_ref, y_ref, s_ref, *work):
    n = g_ref.shape[0]
    rank = rank_ref[0, place()]
    keep = iota((n, n), 1) < rank
    x_ref[...] = m_ref[:n, :n]
    y_ref[...] = m_ref[n:, n:]
    s_ref[...] = m_ref[:n, n:]
    eliminate([x_ref, y_ref])
    px = jnp.where(keep, v_ref[:n, :], 0.0)
    py = jnp.where(keep, v_ref[n:, :], 0.0)
    g_ref[...] = combine(3, x_ref, y_ref, s_ref, px, py, g_ref, work) + unit_rest(n, rank)


def merge_kernel(depth, rank_ref, x_ref, y_ref, mine_ref, theirs_ref, g_ref, s_ref, *work):
    n = g_ref.shape[0]
    rx, ry, rp = rank_at(rank_ref, depth), rank_at(rank_ref, depth, 1), rank_at(rank_ref, depth, 0, 1)
    s_ref[...] = both(n, rx, ry, mine_ref[1] + theirs_ref[1].T)
    px = both(n, rx, rp, mine_ref[0])
    py = both(n, ry, rp, theirs_ref[0])
    g_ref[...] = combine(2, x_ref, y_ref, s_ref, px, py, g_ref, work) + unit_rest(n, rp)


def half_pass(a_ref, keep_ref, reverse, second):
    tiles = a_ref.shape[0] // LANES
    for i in range(tiles // 2, tiles) if second else range(tiles // 2):
        yield from tile_pass(a_ref, keep_ref, reverse, tiles - 1 - i if reverse else i)


def first_kernel(g_ref, half_ref):
    half_ref[...] = g_ref[...]
    together([half_pass(half_ref, None, False, False)])


def middle_kernel(depth, rank_ref, before_ref, g_ref, l_ref, half_ref, a_ref):
    n = g_ref.shape[0]
    a_ref[...] = before_ref[...]
    half_ref[...] = g_ref[...]
    together([half_pass(a_ref, None, False, True), half_pass(half_ref, None, False, False)])
    rank = rank_at(rank_ref, depth - 1)
    l_ref[...] = both(n, rank, rank, a_ref[...])


def factor_of(n, e):
    row, col = iota((n, n), 0), iota((n, n), 1)
    upper = jnp.where(row < col, e, 0.0) + jnp.where(row == col, 1.0 / jnp.where(row == col, e, 1.0), 0.0)
    return upper.T


def group_pair(n, depth, rank_ref):
    pos = lax.axis_index("outer")
    first = jnp.bitwise_and(pos, 1) == 0
    node = jnp.bitwise_and(pos, -2)
    pick = jnp.where(first, 1, 0) + jnp.zeros((n, n), jnp.int32) > 0
    return first, pick, rank_ref[depth, node], rank_ref[depth, node + 1]


def roots_kernel(depth, rank_ref, g_ref, go_ref, c_ref, co_ref, before_ref, *refs):
    n = g_ref.shape[0]
    lower = refs[: depth - 2]
    keep_ref, s_ref, out_ref, l_ref, a_ref, b_ref, h_ref = refs[depth - 2 : depth + 5]
    work = refs[depth + 5 :]
    for i, ref in enumerate(lower):
        out_ref[i] = ref[...]
    first, pick, ra, rb = group_pair(n, depth, rank_ref)
    a_ref[...] = jnp.where(pick, g_ref[...], go_ref[...])
    b_ref[...] = jnp.where(pick, go_ref[...], g_ref[...])
    ca = jnp.where(pick, c_ref[...], co_ref[...])
    cb = jnp.where(pick, co_ref[...], c_ref[...])
    s_ref[...] = both(n, rb, ra, ca.T + cb)
    h_ref[...] = before_ref[...]
    neumann(2, b_ref, a_ref, s_ref, b_ref[...], l_ref, work)
    turned = thirds(s_ref[...])
    back = dot6(thirds(dot6(turned, thirds(a_ref[...]))), turned, nt=True)
    l_ref[...] = jnp.where(pick, 0.0, back)
    a_ref[...] = jnp.where(pick, a_ref[...], work[0][...])
    together([half_pass(a_ref, keep_ref, True, False), half_pass(h_ref, None, False, True)])
    together([half_pass(a_ref, keep_ref, True, True)])
    rank = rank_at(rank_ref, depth - 1)
    out_ref[depth - 2] = both(n, rank, rank, h_ref[...])
    rank = jnp.where(first, ra, rb)
    out_ref[depth - 1] = both(n, rank, rank, a_ref[...] + l_ref[...])


def top_kernel(depth, rank_ref, k_ref, ko_ref, s_ref, f_ref):
    n = k_ref.shape[0]
    _, pick, _, _ = group_pair(n, depth, rank_ref)
    row, col = iota((n, n), 0), iota((n, n), 1)
    e = jnp.where(pick, k_ref[...], ko_ref[...])
    f_ref[:n, :n] = factor_of(n, e)
    f_ref[:n, n:] = jnp.zeros((n, n), jnp.float32)
    f_ref[n:, :n] = dot6(thirds(s_ref[...]), thirds(jnp.where(row >= col, e, 0.0)), nt=True)
    f_ref[n:, n:] = factor_of(n, jnp.where(pick, ko_ref[...], k_ref[...]))


def call(kernel, outs, n, scratch, *arrays, ranks=None, flops=10**9):
    vmem = pl.BlockSpec(memory_space=pltpu.VMEM)
    lead = [] if ranks is None else [pl.BlockSpec(memory_space=pltpu.SMEM)]
    return pl.pallas_call(
        kernel,
        out_shape=[jax.ShapeDtypeStruct(shape, jnp.float32) for shape in outs],
        in_specs=lead + [vmem] * len(arrays),
        out_specs=[vmem] * len(outs),
        scratch_shapes=[pltpu.VMEM((n, n), jnp.float32)] * scratch,
        compiler_params=pltpu.CompilerParams(vmem_limit_bytes=GRANT),
        cost_estimate=pl.CostEstimate(flops=flops, bytes_accessed=4 * 10**6, transcendentals=0),
    )(*([] if ranks is None else [ranks]), *arrays)


def partner(x, axis, bit):
    return lax.ppermute(x, axis, [(i, i ^ 1 << bit) for i in range(lax.axis_size(axis))])


def steps(leaf_blocks, leaf_bases, local_gens, chain_gens, node_ranks):
    n = leaf_bases.shape[2]
    in_levels = chain_gens.shape[0]
    square = (n, n)
    gens = [local_gens[0]]
    others = [partner(gens[0], "inner", 0)]
    g = call(leaf_kernel, [square], n, 7, leaf_blocks[0], leaf_bases[0], ranks=node_ranks, flops=8 * 10**9)[0]
    g_other = partner(g, "inner", 0)
    g, chain_gens = lax.optimization_barrier((g, chain_gens))
    gens = gens + [chain_gens[d] for d in range(in_levels)]
    couple = gens[in_levels][1]
    for d in range(1, in_levels):
        others.append(partner(gens[d], "inner", d))
    other_couple = partner(couple, "outer", 0)
    reduced = []
    half = None
    for depth in range(in_levels):
        if depth == 0:
            half = call(first_kernel, [square], n, 0, g, flops=4 * 10**9)[0]
        else:
            g_other = partner(g, "inner", depth)
            middle = functools.partial(middle_kernel, depth)
            done, half = call(middle, [square] * 2, n, 1, half, g, ranks=node_ranks, flops=4 * 10**9)
            reduced.append(done)
        merge = functools.partial(merge_kernel, depth)
        g = call(merge, [square], n, 5, g, g_other, gens[depth], others[depth], ranks=node_ranks)[0]
    g_other = partner(g, "outer", 0)
    roots = functools.partial(roots_kernel, in_levels)
    arrays = (g, g_other, couple, other_couple, half, *reduced[1:])
    outs = [square, square, (in_levels, n, n)]
    e, s, chain = call(roots, outs, n, 8, *arrays, ranks=node_ranks, flops=4 * 10**9)
    e_other = partner(e, "outer", 0)
    top = functools.partial(top_kernel, in_levels)
    factor = call(top, [(2 * n, 2 * n)], n, 0, e, e_other, s, ranks=node_ranks, flops=4 * 10**9)[0]
    return (reduced[0][None], chain, factor)


def solution(mesh):
    return jax.shard_map(
        steps,
        mesh=mesh,
        in_specs=(
            P(("outer", "inner"), None, None),
            P(("outer", "inner"), None, None),
            P(("outer", "inner"), None, None, None),
            P(("outer", "inner"), None, None, None),
            P(),
        ),
        out_specs=(
            P(("outer", "inner"), None, None),
            P(("outer", "inner"), None, None),
            P(("outer", "inner"), None),
        ),
        check_vma=False,
    )
```

```python
import functools

import jax
import jax.numpy as jnp
from jax import lax
from jax.experimental import pallas as pl
from jax.experimental.pallas import tpu as pltpu
from jax.sharding import PartitionSpec as P

LANES = 128
SUB = 8
PANEL = 32
TOLERANCE = 4e-6
MOST = 40
GRANT = 20 * 2**20
HIGH = lax.Precision.HIGHEST


def dot(a, b, dims=((1,), (0,))):
    return lax.dot_general(a, b, (dims, ((), ())), precision=HIGH, preferred_element_type=jnp.float32)


NT = ((1,), (1,))


def thirds(x):
    a = x.astype(jnp.bfloat16)
    x = x - a.astype(jnp.float32)
    b = x.astype(jnp.bfloat16)
    return a, b, (x - b.astype(jnp.float32)).astype(jnp.bfloat16)


def bdot(a, b):
    return jnp.dot(a, b, preferred_element_type=jnp.float32)


def iota(shape, axis):
    return lax.broadcasted_iota(jnp.int32, shape, axis)


def total(terms):
    while len(terms) > 1:
        terms = [a + b for a, b in zip(terms[::2], terms[1::2])] + terms[len(terms) // 2 * 2 :]
    return terms[0]


def row_of(x, j):
    return jnp.broadcast_to(x[j : j + 1, :], x.shape)


def col_of(x, c):
    return jnp.broadcast_to(x[:, c : c + 1], x.shape)


def tile_pass(a_ref, keep_ref, reverse, h):
    n = a_ref.shape[0]
    tiles = n // LANES
    groups = PANEL // SUB
    sub = iota((SUB, LANES), 0)
    lane = iota((SUB, LANES), 1)
    wide = iota((n, LANES), 1)

    def order(count):
        return range(count - 1, -1, -1) if reverse else range(count)

    own_at = pl.multiple_of(h * LANES, LANES)
    spots = [own_at] + [pl.multiple_of(lax.rem(h + t, tiles) * LANES, LANES) for t in range(1, tiles)]
    ahead = None
    panels = list(order(LANES // PANEL))
    for q in panels:
        base_row = pl.multiple_of(h * LANES + q * PANEL, PANEL)
        rows = [
            [a_ref[pl.ds(pl.multiple_of(base_row + g * SUB, SUB), SUB), pl.ds(spot, LANES)] for spot in spots]
            for g in range(groups)
        ] if ahead is None else ahead
        for s in order(groups):
            c0 = q * PANEL + s * SUB
            cols = [col_of(rows[s][0], c0 + j) for j in range(SUB)]
            other = {g: [col_of(rows[g][0], c0 + j) for j in range(SUB)] for g in range(groups) if g != s}
            piv = list(rows[s])
            kept = [jnp.zeros((SUB, LANES), jnp.float32) for _ in spots]
            left = list(order(SUB))
            inv = 1.0 / row_of(cols[left[0]], left[0])
            yield
            while left:
                j = left.pop(0)
                here = lane == c0 + j
                at = sub == j
                lines = [row_of(x, j) for x in piv]
                if keep_ref is not None:
                    root = lax.rsqrt(row_of(cols[j], j))
                    kept = [jnp.where(at, x * root, k) for x, k in zip(lines, kept)]
                mult = jnp.where(at, -1.0, cols[j])
                now = inv
                if left:
                    i = left[0]
                    cross = row_of(cols[i], j)
                    inv = 1.0 / (row_of(cols[i], i) - (cross * now) * row_of(cols[j], i))
                lines = [jnp.where(here, 1.0, lines[0])] + lines[1:]
                bases = [jnp.where(at | here, 0.0, piv[0])] + [jnp.where(at, 0.0, x) for x in piv[1:]]
                piv = [y - mult * (x * now) for x, y in zip(lines, bases)]
                for i in left:
                    cols[i] = jnp.where(at, 0.0, cols[i]) - mult * (row_of(cols[i], j) * now)
                yield
            rows[s] = piv
            if keep_ref is not None:
                for spot, k in zip(spots, kept):
                    keep_ref[pl.ds(pl.multiple_of(base_row + s * SUB, SUB), SUB), pl.ds(spot, LANES)] = k
            spread = [[row_of(x, j) for j in range(SUB)] for x in piv]
            inside = (lane >= c0) & (lane < c0 + SUB)
            for g, mult in other.items():
                new = list(rows[g])
                new[0] = jnp.where(inside, 0.0, new[0])
                rows[g] = [x - total([mult[j] * y[j] for j in range(SUB)]) for x, y in zip(new, spread)]
                yield
        weights = []
        for t in range(tiles):
            r1, r2, r3 = thirds(jnp.concatenate([rows[g][t] for g in range(groups)], axis=0))
            blank = jnp.zeros((LANES - 2 * PANEL, LANES), jnp.bfloat16)
            weights.append(jnp.concatenate([r1, r1, r2, r2, r1, r3, blank], axis=0))
        yield

        def updated(at, count):
            inside = (wide[:count] >= q * PANEL) & (wide[:count] < (q + 1) * PANEL)
            own = a_ref[pl.ds(at, count), pl.ds(own_at, LANES)]
            olds = [jnp.where(inside, 0.0, own)] + [a_ref[pl.ds(at, count), pl.ds(spot, LANES)] for spot in spots[1:]]
            x = jnp.where(inside, own, 0.0)
            x = x + pltpu.roll(x, PANEL, 1)
            x = x + pltpu.roll(x, 2 * PANEL, 1)
            l1 = x.astype(jnp.bfloat16).astype(jnp.float32)
            l2 = (x - l1).astype(jnp.bfloat16).astype(jnp.float32)
            l3 = x - l1 - l2
            at_quarter = wide[:count] // PANEL
            one = jnp.where((at_quarter & 1) == 0, l1, l2)
            two = jnp.where(at_quarter == 0, l3, jnp.where(at_quarter == 1, l1, 0.0))
            lhs = jnp.concatenate([one.astype(jnp.bfloat16), two.astype(jnp.bfloat16)], axis=1)
            return [old - bdot(lhs, w) for old, w in zip(olds, weights)]

        ahead = None
        if q != panels[-1]:
            onward = -PANEL if reverse else PANEL
            block = updated(pl.multiple_of(base_row + onward, PANEL), PANEL)
            ahead = [[x[g * SUB : (g + 1) * SUB] for x in block] for g in range(groups)]
        yield
        for spot, x in zip(spots, updated(0, n)):
            a_ref[:, pl.ds(spot, LANES)] = x
        for g in range(groups):
            for spot, x in zip(spots, rows[g]):
                a_ref[pl.ds(pl.multiple_of(base_row + g * SUB, SUB), SUB), pl.ds(spot, LANES)] = x
        yield


def together(passes):
    while passes:
        passes = [p for p in passes if next(p, passes) is not passes]


def eliminate(refs, keeps=None, reverse=False):
    tiles = refs[0].shape[0] // LANES
    keeps = keeps or [None] * len(refs)

    def step(i, carry):
        h = tiles - 1 - i if reverse else i
        together([tile_pass(a, k, reverse, h) for a, k in zip(refs, keeps)])
        return carry

    lax.fori_loop(0, tiles, step, 0)


def segment_col(x, c):
    at = iota(x.shape, 1) // PANEL * PANEL + c
    return jnp.take_along_axis(x, at, axis=1, mode="promise_in_bounds")


def base_pass(a_ref, start, out):
    groups = PANEL // SUB
    sub = iota((SUB, LANES), 0)
    lane = iota((SUB, LANES), 1)
    segment, spot = lane // PANEL, lane % PANEL
    rows = []
    for g in range(groups):
        row = jnp.zeros((SUB, LANES), jnp.float32)
        for b in range(LANES // PANEL):
            part = a_ref[start + b * PANEL + g * SUB : start + b * PANEL + (g + 1) * SUB, start : start + LANES]
            row = jnp.where(segment == b, part, row)
        rows.append(row)
    for s in range(groups):
        c0 = s * SUB
        cols = [segment_col(rows[s], c0 + j) for j in range(SUB)]
        other = {g: [segment_col(rows[g], c0 + j) for j in range(SUB)] for g in range(groups) if g != s}
        piv = rows[s]
        inv = 1.0 / row_of(cols[0], 0)
        yield
        for j in range(SUB):
            here = spot == c0 + j
            at = sub == j
            line = row_of(piv, j)
            mult = jnp.where(at, -1.0, cols[j])
            now = inv
            if j + 1 < SUB:
                i = j + 1
                inv = 1.0 / (row_of(cols[i], i) - (row_of(cols[i], j) * now) * row_of(cols[j], i))
            line = jnp.where(here, 1.0, line)
            piv = jnp.where(at | here, 0.0, piv) - mult * (line * now)
            for i in range(j + 1, SUB):
                cols[i] = jnp.where(at, 0.0, cols[i]) - mult * (row_of(cols[i], j) * now)
            yield
        rows[s] = piv
        spread = [row_of(piv, j) for j in range(SUB)]
        inside = (spot >= c0) & (spot < c0 + SUB)
        for g, mult in other.items():
            rows[g] = jnp.where(inside, 0.0, rows[g]) - total([m * y for m, y in zip(mult, spread)])
        yield
    out.append(jnp.concatenate([jnp.where(segment == b, r, 0.0) for b in range(LANES // PANEL) for r in rows], axis=0))
    yield


def level_pass(a_ref, start, size, before, out, rests):
    row, col = iota((LANES, LANES), 0), iota((LANES, LANES), 1)
    across = (row // (2 * size) == col // (2 * size)) & (row // size != col // size)
    couple = jnp.where(across, a_ref[start : start + LANES, start : start + LANES], 0.0)
    split = thirds(before)
    e = thirds(dot6(split, thirds(couple)))
    yield
    x = before - dot6(e, split)
    power = thirds(dot3(e, e))
    yield
    x = x + dot3(power, thirds(x))
    power = thirds(dot3(power, power))
    yield
    out.append(x + dot3(power, thirds(x)))
    rests.append(bdot(power[0], power[0]))
    yield


def join_pass(a_ref, x, y, out_ref, rests):
    b, xs, ys = thirds(a_ref[:LANES, LANES:]), thirds(x), thirds(y)
    u = thirds(dot6(xs, b))
    v = thirds(dot3(ys, b, nt=True))
    yield
    power = thirds(dot3(v, u))
    yield
    z = y + dot3(power, ys)
    power = thirds(dot3(power, power))
    yield
    z = z + dot3(power, thirds(z))
    power = thirds(dot3(power, power))
    yield
    z = z + dot3(power, thirds(z))
    rests.append(bdot(power[0], power[0]))
    yield
    w = dot6(u, thirds(z))
    yield
    out_ref[:LANES, :LANES] = x + dot6(thirds(w), u, nt=True)
    out_ref[:LANES, LANES:] = -w
    out_ref[LANES:, :LANES] = -w.T
    out_ref[LANES:, LANES:] = z
    yield


def invert_pair(a_ref, out_ref):
    count, n = a_ref.shape[0], a_ref.shape[1]
    spots = [(i, t * LANES) for i in range(count) for t in range(n // LANES)]
    found = [[] for _ in spots]
    rests = []
    together([base_pass(a_ref.at[i], at, f) for (i, at), f in zip(spots, found)])
    size = PANEL
    while size < LANES:
        together([level_pass(a_ref.at[i], at, size, f[-1], f, rests) for (i, at), f in zip(spots, found)])
        size = 2 * size
    together([join_pass(a_ref.at[i], found[2 * i][-1], found[2 * i + 1][-1], out_ref.at[i], rests) for i in range(count)])
    rest = total([r * r for r in rests])

    @pl.when(jnp.logical_not(jnp.sum(rest) <= TOLERANCE * TOLERANCE))
    def _():
        out_ref[...] = a_ref[...]

        def direct(i, carry):
            eliminate([out_ref.at[i]])
            return carry

        lax.fori_loop(0, count, direct, 0)


def unit_rest(n, rank):
    return jnp.where((iota((n, n), 0) == iota((n, n), 1)) & (iota((n, n), 0) >= rank), 1.0, 0.0)


def both(n, rank_row, rank_col, x):
    return jnp.where((iota((n, n), 0) < rank_row) & (iota((n, n), 1) < rank_col), x, 0.0)


def place():
    return lax.axis_index("outer") * lax.axis_size("inner") + lax.axis_index("inner")


def rank_at(rank_ref, depth, flip=0, up=0):
    return rank_ref[depth + up, jnp.bitwise_xor(jnp.right_shift(place(), depth + up), flip)]


def product(a, b, nt=False):
    return lax.dot_general(a, b, (NT if nt else ((1,), (0,)), ((), ())), preferred_element_type=jnp.float32)


def dot6(a, b, nt=False):
    (a1, a2, a3), (b1, b2, b3) = a, b
    axis = 1 if nt else 0
    small = product(jnp.concatenate([a2, a1, a3], axis=1), jnp.concatenate([b2, b3, b1], axis=axis), nt)
    large = product(jnp.concatenate([a2, a1, a1], axis=1), jnp.concatenate([b1, b2, b1], axis=axis), nt)
    return small + large


def dot3(a, b, nt=False):
    axis = 1 if nt else 0
    small = product(jnp.concatenate([a[1], a[0]], axis=1), jnp.concatenate([b[0], b[1]], axis=axis), nt)
    return small + product(a[0], b[0], nt)


def slow_dot(out_ref, a_ref, b_ref, dims=((1,), (0,)), add=False):
    n = out_ref.shape[0]

    def rows(i, carry):
        at = pl.ds(pl.multiple_of(i * PANEL, PANEL), PANEL)
        x = dot(a_ref[at, :], b_ref[...], dims)
        out_ref[at, :] = x + b_ref[at, :] if add else x
        return carry

    lax.fori_loop(0, n // PANEL, rows, 0)


def square_sum(x):
    return jnp.sum(x * x)


def neumann(steps, x_ref, y_ref, s_ref, z, hold_ref, work):
    z_ref, p_ref, q_ref, w_ref = work
    s = thirds(s_ref[...])
    a = dot3(thirds(x_ref[...]), s)
    u = dot3(s, thirds(y_ref[...]))
    power = thirds(dot3(thirds(a), thirds(u), nt=True))
    hold_ref[...] = z
    z = z + dot3(power, thirds(z))
    for _ in range(steps - 1):
        raised = dot3(power, power)
        power = thirds(raised)
        z = z + dot3(power, thirds(z))
    z_ref[...] = z

    @pl.when(jnp.logical_not(square_sum(raised) <= TOLERANCE))
    def _():
        slow_dot(p_ref, x_ref, s_ref)
        slow_dot(q_ref, s_ref, y_ref)
        slow_dot(w_ref, p_ref, q_ref, NT)
        z_ref[...] = hold_ref[...]

        def more(carry):
            count, rest = carry
            return (count < MOST) & (rest > TOLERANCE)

        def raise_power(carry):
            count, _ = carry
            slow_dot(p_ref, w_ref, z_ref, add=True)
            z_ref[...] = p_ref[...]
            slow_dot(q_ref, w_ref, w_ref)
            rest = square_sum(w_ref[...])
            w_ref[...] = q_ref[...]
            return count + 1, rest

        lax.while_loop(more, raise_power, (jnp.int32(0), jnp.float32(1.0)))


def combine(steps, x_ref, y_ref, s_ref, px, py, g_ref, work):
    py3 = thirds(py)
    t = thirds(dot6(thirds(y_ref[...]), py3))
    y = px - dot6(thirds(s_ref[...]), t)
    z = dot6(thirds(x_ref[...]), thirds(y))
    g = dot6(thirds(py.T), t)
    turned = y.T
    neumann(steps, x_ref, y_ref, s_ref, z, g_ref, work)
    return g + dot6(thirds(turned), thirds(work[0][...]))


def leaf_kernel(rank_ref, m_ref, v_ref, g_ref, a_ref, xy_ref, vv_ref, sem, s_ref, *work):
    n = g_ref.shape[0]
    moves = [
        (m_ref.at[:n, :n], a_ref.at[0]),
        (m_ref.at[n:, n:], a_ref.at[1]),
        (m_ref.at[:n, n:], s_ref),
        (v_ref, vv_ref),
    ]
    copies = [pltpu.make_async_copy(src, dst, sem.at[i]) for i, (src, dst) in enumerate(moves)]
    for copy in copies:
        copy.start()
    rank = rank_ref[0, place()]
    keep = iota((n, n), 1) < rank
    copies[0].wait()
    copies[1].wait()
    if n == 2 * LANES:
        invert_pair(a_ref, xy_ref)
    else:
        xy_ref[...] = a_ref[...]
        eliminate([xy_ref.at[0], xy_ref.at[1]])
    copies[2].wait()
    copies[3].wait()
    px = jnp.where(keep, vv_ref[:n, :], 0.0)
    py = jnp.where(keep, vv_ref[n:, :], 0.0)
    g_ref[...] = combine(3, xy_ref.at[0], xy_ref.at[1], s_ref, px, py, g_ref, work) + unit_rest(n, rank)


def merge_kernel(depth, rank_ref, x_ref, y_ref, mine_ref, theirs_ref, g_ref, s_ref, *work):
    n = g_ref.shape[0]
    rx, ry, rp = rank_at(rank_ref, depth), rank_at(rank_ref, depth, 1), rank_at(rank_ref, depth, 0, 1)
    s_ref[...] = both(n, rx, ry, mine_ref[1] + theirs_ref[1].T)
    px = both(n, rx, rp, mine_ref[0])
    py = both(n, ry, rp, theirs_ref[0])
    g_ref[...] = combine(2, x_ref, y_ref, s_ref, px, py, g_ref, work) + unit_rest(n, rp)


def half_pass(a_ref, keep_ref, reverse, second):
    tiles = a_ref.shape[0] // LANES
    for i in range(tiles // 2, tiles) if second else range(tiles // 2):
        yield from tile_pass(a_ref, keep_ref, reverse, tiles - 1 - i if reverse else i)


def first_kernel(g_ref, half_ref):
    half_ref[...] = g_ref[...]
    together([half_pass(half_ref, None, False, False)])


def middle_kernel(depth, rank_ref, before_ref, g_ref, l_ref, half_ref, a_ref):
    n = g_ref.shape[0]
    a_ref[...] = before_ref[...]
    half_ref[...] = g_ref[...]
    together([half_pass(a_ref, None, False, True), half_pass(half_ref, None, False, False)])
    rank = rank_at(rank_ref, depth - 1)
    l_ref[...] = both(n, rank, rank, a_ref[...])


def factor_of(n, e):
    row, col = iota((n, n), 0), iota((n, n), 1)
    upper = jnp.where(row < col, e, 0.0) + jnp.where(row == col, 1.0 / jnp.where(row == col, e, 1.0), 0.0)
    return upper.T


def group_pair(n, depth, rank_ref):
    pos = lax.axis_index("outer")
    first = jnp.bitwise_and(pos, 1) == 0
    node = jnp.bitwise_and(pos, -2)
    pick = jnp.where(first, 1, 0) + jnp.zeros((n, n), jnp.int32) > 0
    return first, pick, rank_ref[depth, node], rank_ref[depth, node + 1]


def roots_kernel(depth, rank_ref, g_ref, go_ref, c_ref, co_ref, before_ref, *refs):
    n = g_ref.shape[0]
    lower = refs[: depth - 2]
    keep_ref, s_ref, out_ref, l_ref, a_ref, b_ref, h_ref = refs[depth - 2 : depth + 5]
    work = refs[depth + 5 :]
    for i, ref in enumerate(lower):
        out_ref[i] = ref[...]
    first, pick, ra, rb = group_pair(n, depth, rank_ref)
    a_ref[...] = jnp.where(pick, g_ref[...], go_ref[...])
    b_ref[...] = jnp.where(pick, go_ref[...], g_ref[...])
    ca = jnp.where(pick, c_ref[...], co_ref[...])
    cb = jnp.where(pick, co_ref[...], c_ref[...])
    s_ref[...] = both(n, rb, ra, ca.T + cb)
    h_ref[...] = before_ref[...]
    neumann(2, b_ref, a_ref, s_ref, b_ref[...], l_ref, work)
    turned = thirds(s_ref[...])
    back = dot6(thirds(dot6(turned, thirds(a_ref[...]))), turned, nt=True)
    l_ref[...] = jnp.where(pick, 0.0, back)
    a_ref[...] = jnp.where(pick, a_ref[...], work[0][...])
    together([half_pass(a_ref, keep_ref, True, False), half_pass(h_ref, None, False, True)])
    together([half_pass(a_ref, keep_ref, True, True)])
    rank = rank_at(rank_ref, depth - 1)
    out_ref[depth - 2] = both(n, rank, rank, h_ref[...])
    rank = jnp.where(first, ra, rb)
    out_ref[depth - 1] = both(n, rank, rank, a_ref[...] + l_ref[...])


def top_kernel(depth, rank_ref, k_ref, ko_ref, s_ref, f_ref):
    n = k_ref.shape[0]
    _, pick, _, _ = group_pair(n, depth, rank_ref)
    row, col = iota((n, n), 0), iota((n, n), 1)
    e = jnp.where(pick, k_ref[...], ko_ref[...])
    f_ref[:n, :n] = factor_of(n, e)
    f_ref[:n, n:] = jnp.zeros((n, n), jnp.float32)
    f_ref[n:, :n] = dot6(thirds(s_ref[...]), thirds(jnp.where(row >= col, e, 0.0)), nt=True)
    f_ref[n:, n:] = factor_of(n, jnp.where(pick, ko_ref[...], k_ref[...]))


def call(kernel, outs, n, scratch, *arrays, ranks=None, flops=10**9, held=(), space=pltpu.VMEM):
    vmem = pl.BlockSpec(memory_space=pltpu.VMEM)
    lead = [] if ranks is None else [pl.BlockSpec(memory_space=pltpu.SMEM)]
    return pl.pallas_call(
        kernel,
        out_shape=[jax.ShapeDtypeStruct(shape, jnp.float32) for shape in outs],
        in_specs=lead + [pl.BlockSpec(memory_space=space)] * len(arrays),
        out_specs=[vmem] * len(outs),
        scratch_shapes=[*held, *[pltpu.VMEM((n, n), jnp.float32)] * scratch],
        compiler_params=pltpu.CompilerParams(vmem_limit_bytes=GRANT),
        cost_estimate=pl.CostEstimate(flops=flops, bytes_accessed=4 * 10**6, transcendentals=0),
    )(*([] if ranks is None else [ranks]), *arrays)


def partner(x, axis, bit):
    return lax.ppermute(x, axis, [(i, i ^ 1 << bit) for i in range(lax.axis_size(axis))])


def steps(leaf_blocks, leaf_bases, local_gens, chain_gens, node_ranks):
    n = leaf_bases.shape[2]
    in_levels = chain_gens.shape[0]
    square = (n, n)
    gens = [local_gens[0]]
    others = [partner(gens[0], "inner", 0)]
    pair = pltpu.VMEM((2, n, n), jnp.float32)
    held = (pair, pair, pltpu.VMEM((2 * n, n), jnp.float32), pltpu.SemaphoreType.DMA((4,)))
    arrays = (leaf_blocks[0], leaf_bases[0])
    g = call(leaf_kernel, [square], n, 5, *arrays, ranks=node_ranks, flops=8 * 10**9, held=held, space=pltpu.HBM)[0]
    g_other = partner(g, "inner", 0)
    g, chain_gens = lax.optimization_barrier((g, chain_gens))
    gens = gens + [chain_gens[d] for d in range(in_levels)]
    couple = gens[in_levels][1]
    for d in range(1, in_levels):
        others.append(partner(gens[d], "inner", d))
    other_couple = partner(couple, "outer", 0)
    reduced = []
    half = None
    for depth in range(in_levels):
        if depth == 0:
            half = call(first_kernel, [square], n, 0, g, flops=4 * 10**9)[0]
        else:
            g_other = partner(g, "inner", depth)
            middle = functools.partial(middle_kernel, depth)
            done, half = call(middle, [square] * 2, n, 1, half, g, ranks=node_ranks, flops=4 * 10**9)
            reduced.append(done)
        merge = functools.partial(merge_kernel, depth)
        g = call(merge, [square], n, 5, g, g_other, gens[depth], others[depth], ranks=node_ranks)[0]
    g_other = partner(g, "outer", 0)
    roots = functools.partial(roots_kernel, in_levels)
    arrays = (g, g_other, couple, other_couple, half, *reduced[1:])
    outs = [square, square, (in_levels, n, n)]
    e, s, chain = call(roots, outs, n, 8, *arrays, ranks=node_ranks, flops=4 * 10**9)
    e_other = partner(e, "outer", 0)
    top = functools.partial(top_kernel, in_levels)
    factor = call(top, [(2 * n, 2 * n)], n, 0, e, e_other, s, ranks=node_ranks, flops=4 * 10**9)[0]
    return (reduced[0][None], chain, factor)


def solution(mesh):
    return jax.shard_map(
        steps,
        mesh=mesh,
        in_specs=(
            P(("outer", "inner"), None, None),
            P(("outer", "inner"), None, None),
            P(("outer", "inner"), None, None, None),
            P(("outer", "inner"), None, None, None),
            P(),
        ),
        out_specs=(
            P(("outer", "inner"), None, None),
            P(("outer", "inner"), None, None),
            P(("outer", "inner"), None),
        ),
        check_vma=False,
    )
```

```python
import functools

import jax
import jax.numpy as jnp
from jax import lax
from jax.experimental import pallas as pl
from jax.experimental.pallas import tpu as pltpu
from jax.sharding import PartitionSpec as P

LANES = 128
SUB = 8
PANEL = 32
TOLERANCE = 4e-6
MOST = 40
LOWEST = -3.4e38
GRANT = 20 * 2**20
WHOLE = 66_700_000
HIGH = lax.Precision.HIGHEST


def dot(a, b, dims=((1,), (0,))):
    return lax.dot_general(a, b, (dims, ((), ())), precision=HIGH, preferred_element_type=jnp.float32)


NT = ((1,), (1,))


def thirds(x):
    a = x.astype(jnp.bfloat16)
    x = x - a.astype(jnp.float32)
    b = x.astype(jnp.bfloat16)
    return a, b, (x - b.astype(jnp.float32)).astype(jnp.bfloat16)


def bdot(a, b):
    return jnp.dot(a, b, preferred_element_type=jnp.float32)


def iota(shape, axis):
    return lax.broadcasted_iota(jnp.int32, shape, axis)


def total(terms):
    while len(terms) > 1:
        terms = [a + b for a, b in zip(terms[::2], terms[1::2])] + terms[len(terms) // 2 * 2 :]
    return terms[0]


def row_of(x, j):
    return jnp.broadcast_to(x[j : j + 1, :], x.shape)


def col_of(x, c):
    return jnp.broadcast_to(x[:, c : c + 1], x.shape)


def tile_pass(a_ref, keep_ref, reverse, h):
    n = a_ref.shape[0]
    tiles = n // LANES
    groups = PANEL // SUB
    sub = iota((SUB, LANES), 0)
    lane = iota((SUB, LANES), 1)
    wide = iota((n, LANES), 1)

    def order(count):
        return range(count - 1, -1, -1) if reverse else range(count)

    own_at = pl.multiple_of(h * LANES, LANES)
    spots = [own_at] + [pl.multiple_of(lax.rem(h + t, tiles) * LANES, LANES) for t in range(1, tiles)]
    ahead = None
    panels = list(order(LANES // PANEL))
    for q in panels:
        base_row = pl.multiple_of(h * LANES + q * PANEL, PANEL)
        rows = [
            [a_ref[pl.ds(pl.multiple_of(base_row + g * SUB, SUB), SUB), pl.ds(spot, LANES)] for spot in spots]
            for g in range(groups)
        ] if ahead is None else ahead
        for s in order(groups):
            c0 = q * PANEL + s * SUB
            cols = [col_of(rows[s][0], c0 + j) for j in range(SUB)]
            other = {g: [col_of(rows[g][0], c0 + j) for j in range(SUB)] for g in range(groups) if g != s}
            piv = list(rows[s])
            kept = [jnp.zeros((SUB, LANES), jnp.float32) for _ in spots]
            left = list(order(SUB))
            inv = 1.0 / row_of(cols[left[0]], left[0])
            yield
            while left:
                j = left.pop(0)
                here = lane == c0 + j
                at = sub == j
                lines = [row_of(x, j) for x in piv]
                if keep_ref is not None:
                    root = lax.rsqrt(row_of(cols[j], j))
                    kept = [jnp.where(at, x * root, k) for x, k in zip(lines, kept)]
                mult = jnp.where(at, -1.0, cols[j])
                now = inv
                if left:
                    i = left[0]
                    cross = row_of(cols[i], j)
                    inv = 1.0 / (row_of(cols[i], i) - (cross * now) * row_of(cols[j], i))
                lines = [jnp.where(here, 1.0, lines[0])] + lines[1:]
                bases = [jnp.where(at | here, 0.0, piv[0])] + [jnp.where(at, 0.0, x) for x in piv[1:]]
                piv = [y - mult * (x * now) for x, y in zip(lines, bases)]
                for i in left:
                    cols[i] = jnp.where(at, 0.0, cols[i]) - mult * (row_of(cols[i], j) * now)
                yield
            rows[s] = piv
            if keep_ref is not None:
                for spot, k in zip(spots, kept):
                    keep_ref[pl.ds(pl.multiple_of(base_row + s * SUB, SUB), SUB), pl.ds(spot, LANES)] = k
            spread = [[row_of(x, j) for j in range(SUB)] for x in piv]
            inside = (lane >= c0) & (lane < c0 + SUB)
            for g, mult in other.items():
                new = list(rows[g])
                new[0] = jnp.where(inside, 0.0, new[0])
                rows[g] = [x - total([mult[j] * y[j] for j in range(SUB)]) for x, y in zip(new, spread)]
                yield
        weights = []
        for t in range(tiles):
            r1, r2, r3 = thirds(jnp.concatenate([rows[g][t] for g in range(groups)], axis=0))
            blank = jnp.zeros((LANES - 2 * PANEL, LANES), jnp.bfloat16)
            weights.append(jnp.concatenate([r1, r1, r2, r2, r1, r3, blank], axis=0))
        yield

        def updated(at, count):
            inside = (wide[:count] >= q * PANEL) & (wide[:count] < (q + 1) * PANEL)
            own = a_ref[pl.ds(at, count), pl.ds(own_at, LANES)]
            olds = [jnp.where(inside, 0.0, own)] + [a_ref[pl.ds(at, count), pl.ds(spot, LANES)] for spot in spots[1:]]
            x = jnp.where(inside, own, 0.0)
            x = x + pltpu.roll(x, PANEL, 1)
            x = x + pltpu.roll(x, 2 * PANEL, 1)
            l1 = x.astype(jnp.bfloat16).astype(jnp.float32)
            l2 = (x - l1).astype(jnp.bfloat16).astype(jnp.float32)
            l3 = x - l1 - l2
            at_quarter = wide[:count] // PANEL
            one = jnp.where((at_quarter & 1) == 0, l1, l2)
            two = jnp.where(at_quarter == 0, l3, jnp.where(at_quarter == 1, l1, 0.0))
            lhs = jnp.concatenate([one.astype(jnp.bfloat16), two.astype(jnp.bfloat16)], axis=1)
            return [old - bdot(lhs, w) for old, w in zip(olds, weights)]

        ahead = None
        if q != panels[-1]:
            onward = -PANEL if reverse else PANEL
            block = updated(pl.multiple_of(base_row + onward, PANEL), PANEL)
            ahead = [[x[g * SUB : (g + 1) * SUB] for x in block] for g in range(groups)]
        yield
        for spot, x in zip(spots, updated(0, n)):
            a_ref[:, pl.ds(spot, LANES)] = x
        for g in range(groups):
            for spot, x in zip(spots, rows[g]):
                a_ref[pl.ds(pl.multiple_of(base_row + g * SUB, SUB), SUB), pl.ds(spot, LANES)] = x
        yield


def together(passes):
    while passes:
        passes = [p for p in passes if next(p, passes) is not passes]


def eliminate(refs, keeps=None, reverse=False):
    tiles = refs[0].shape[0] // LANES
    keeps = keeps or [None] * len(refs)

    def step(i, carry):
        h = tiles - 1 - i if reverse else i
        together([tile_pass(a, k, reverse, h) for a, k in zip(refs, keeps)])
        return carry

    lax.fori_loop(0, tiles, step, 0)


def segment_col(x, c):
    at = iota(x.shape, 1) // PANEL * PANEL + c
    return jnp.take_along_axis(x, at, axis=1, mode="promise_in_bounds")


def base_pass(a_ref, start, out):
    groups = PANEL // SUB
    sub = iota((SUB, LANES), 0)
    lane = iota((SUB, LANES), 1)
    segment, spot = lane // PANEL, lane % PANEL
    rows = []
    for g in range(groups):
        row = jnp.zeros((SUB, LANES), jnp.float32)
        for b in range(LANES // PANEL):
            part = a_ref[start + b * PANEL + g * SUB : start + b * PANEL + (g + 1) * SUB, start : start + LANES]
            row = jnp.where(segment == b, part, row)
        rows.append(row)
    for s in range(groups):
        c0 = s * SUB
        cols = [segment_col(rows[s], c0 + j) for j in range(SUB)]
        other = {g: [segment_col(rows[g], c0 + j) for j in range(SUB)] for g in range(groups) if g != s}
        piv = rows[s]
        inv = 1.0 / row_of(cols[0], 0)
        yield
        for j in range(SUB):
            here = spot == c0 + j
            at = sub == j
            line = row_of(piv, j)
            mult = jnp.where(at, -1.0, cols[j])
            now = inv
            if j + 1 < SUB:
                i = j + 1
                inv = 1.0 / (row_of(cols[i], i) - (row_of(cols[i], j) * now) * row_of(cols[j], i))
            line = jnp.where(here, 1.0, line)
            piv = jnp.where(at | here, 0.0, piv) - mult * (line * now)
            for i in range(j + 1, SUB):
                cols[i] = jnp.where(at, 0.0, cols[i]) - mult * (row_of(cols[i], j) * now)
            yield
        rows[s] = piv
        spread = [row_of(piv, j) for j in range(SUB)]
        inside = (spot >= c0) & (spot < c0 + SUB)
        for g, mult in other.items():
            rows[g] = jnp.where(inside, 0.0, rows[g]) - total([m * y for m, y in zip(mult, spread)])
        yield
    out.append(jnp.concatenate([jnp.where(segment == b, r, 0.0) for b in range(LANES // PANEL) for r in rows], axis=0))
    yield


def level_pass(a_ref, start, size, before, out, rests):
    row, col = iota((LANES, LANES), 0), iota((LANES, LANES), 1)
    across = (row // (2 * size) == col // (2 * size)) & (row // size != col // size)
    couple = jnp.where(across, a_ref[start : start + LANES, start : start + LANES], 0.0)
    split = thirds(before)
    e = thirds(dot6(split, thirds(couple)))
    yield
    x = before - dot6(e, split)
    power = thirds(dot3(e, e))
    yield
    x = x + dot3(power, thirds(x))
    power = thirds(dot3(power, power))
    yield
    out.append(x + dot3(power, thirds(x)))
    rests.append(bdot(power[0], power[0]))
    yield


def join_pass(a_ref, x, y, out_ref, rests):
    b, xs, ys = thirds(a_ref[:LANES, LANES:]), thirds(x), thirds(y)
    u = thirds(dot6(xs, b))
    v = thirds(dot3(ys, b, nt=True))
    yield
    power = thirds(dot3(v, u))
    yield
    z = y + dot3(power, ys)
    power = thirds(dot3(power, power))
    yield
    z = z + dot3(power, thirds(z))
    power = thirds(dot3(power, power))
    yield
    z = z + dot3(power, thirds(z))
    rests.append(bdot(power[0], power[0]))
    yield
    w = dot6(u, thirds(z))
    yield
    out_ref[:LANES, :LANES] = x + dot6(thirds(w), u, nt=True)
    out_ref[:LANES, LANES:] = -w
    out_ref[LANES:, :LANES] = -w.T
    out_ref[LANES:, LANES:] = z
    yield


def invert_pair(a_ref, out_ref):
    count, n = a_ref.shape[0], a_ref.shape[1]
    spots = [(i, t * LANES) for i in range(count) for t in range(n // LANES)]
    found = [[] for _ in spots]
    rests = []
    together([base_pass(a_ref.at[i], at, f) for (i, at), f in zip(spots, found)])
    size = PANEL
    while size < LANES:
        together([level_pass(a_ref.at[i], at, size, f[-1], f, rests) for (i, at), f in zip(spots, found)])
        size = 2 * size
    together([join_pass(a_ref.at[i], found[2 * i][-1], found[2 * i + 1][-1], out_ref.at[i], rests) for i in range(count)])
    rest = total([r * r for r in rests])

    @pl.when(jnp.logical_not(jnp.sum(rest) <= TOLERANCE * TOLERANCE))
    def _():
        out_ref[...] = a_ref[...]

        def direct(i, carry):
            eliminate([out_ref.at[i]])
            return carry

        lax.fori_loop(0, count, direct, 0)


def unit_rest(n, rank):
    return jnp.where((iota((n, n), 0) == iota((n, n), 1)) & (iota((n, n), 0) >= rank), 1.0, 0.0)


def both(n, rank_row, rank_col, x):
    return jnp.where((iota((n, n), 0) < rank_row) & (iota((n, n), 1) < rank_col), x, 0.0)


def place():
    return lax.axis_index("outer") * lax.axis_size("inner") + lax.axis_index("inner")


def rank_at(rank_ref, depth, flip=0, up=0):
    return rank_ref[depth + up, jnp.bitwise_xor(jnp.right_shift(place(), depth + up), flip)]


def product(a, b, nt=False):
    return lax.dot_general(a, b, (NT if nt else ((1,), (0,)), ((), ())), preferred_element_type=jnp.float32)


def dot6(a, b, nt=False):
    (a1, a2, a3), (b1, b2, b3) = a, b
    axis = 1 if nt else 0
    small = product(jnp.concatenate([a2, a1, a3], axis=1), jnp.concatenate([b2, b3, b1], axis=axis), nt)
    large = product(jnp.concatenate([a2, a1, a1], axis=1), jnp.concatenate([b1, b2, b1], axis=axis), nt)
    return apart(small) + large


def dot3(a, b, nt=False):
    axis = 1 if nt else 0
    small = product(jnp.concatenate([a[1], a[0]], axis=1), jnp.concatenate([b[0], b[1]], axis=axis), nt)
    return apart(small) + product(a[0], b[0], nt)


def apart(x):
    return jnp.maximum(x, LOWEST) if x.shape[0] > LANES else x


def slow_dot(out_ref, a_ref, b_ref, dims=((1,), (0,)), add=False):
    n = out_ref.shape[0]

    def rows(i, carry):
        at = pl.ds(pl.multiple_of(i * PANEL, PANEL), PANEL)
        x = dot(a_ref[at, :], b_ref[...], dims)
        out_ref[at, :] = x + b_ref[at, :] if add else x
        return carry

    lax.fori_loop(0, n // PANEL, rows, 0)


def square_sum(x):
    return jnp.sum(x * x)


def first_power(x_ref, y_ref, s_ref):
    s = thirds(s_ref[...])
    a = dot3(thirds(x_ref[...]), s)
    u = dot3(s, thirds(y_ref[...]))
    return thirds(dot3(thirds(a), thirds(u), nt=True))


def neumann(steps, power, x_ref, y_ref, s_ref, z, hold_ref, work):
    z_ref, p_ref, q_ref, w_ref = work
    hold_ref[...] = z
    z = z + dot3(power, thirds(z))
    for _ in range(steps - 1):
        raised = dot3(power, power)
        power = thirds(raised)
        z = z + dot3(power, thirds(z))
    z_ref[...] = z

    @pl.when(jnp.logical_not(square_sum(raised) <= TOLERANCE))
    def _():
        slow_dot(p_ref, x_ref, s_ref)
        slow_dot(q_ref, s_ref, y_ref)
        slow_dot(w_ref, p_ref, q_ref, NT)
        z_ref[...] = hold_ref[...]

        def more(carry):
            count, rest = carry
            return (count < MOST) & (rest > TOLERANCE)

        def raise_power(carry):
            count, _ = carry
            slow_dot(p_ref, w_ref, z_ref, add=True)
            z_ref[...] = p_ref[...]
            slow_dot(q_ref, w_ref, w_ref)
            rest = square_sum(w_ref[...])
            w_ref[...] = q_ref[...]
            return count + 1, rest

        lax.while_loop(more, raise_power, (jnp.int32(0), jnp.float32(1.0)))


def combine(steps, x_ref, y_ref, s_ref, px, py, g_ref, work):
    py3 = thirds(py)
    t = thirds(dot6(thirds(y_ref[...]), py3))
    power = first_power(x_ref, y_ref, s_ref)
    y = px - dot6(thirds(s_ref[...]), t)
    z = dot6(thirds(x_ref[...]), thirds(y))
    g = dot6(thirds(py.T), t)
    turned = y.T
    neumann(steps, power, x_ref, y_ref, s_ref, z, g_ref, work)
    return g + dot6(thirds(turned), thirds(work[0][...]))


def leaf_kernel(rank_ref, m_ref, v_ref, g_ref, a_ref, xy_ref, vv_ref, sem, s_ref, *work):
    n = g_ref.shape[0]
    moves = [
        (m_ref.at[:n, :n], a_ref.at[0]),
        (m_ref.at[n:, n:], a_ref.at[1]),
        (m_ref.at[:n, n:], s_ref),
        (v_ref, vv_ref),
    ]
    copies = [pltpu.make_async_copy(src, dst, sem.at[i]) for i, (src, dst) in enumerate(moves)]
    for copy in copies:
        copy.start()
    rank = rank_ref[0, place()]
    keep = iota((n, n), 1) < rank
    copies[0].wait()
    copies[1].wait()
    if n == 2 * LANES:
        invert_pair(a_ref, xy_ref)
    else:
        xy_ref[...] = a_ref[...]
        eliminate([xy_ref.at[0], xy_ref.at[1]])
    copies[2].wait()
    copies[3].wait()
    px = jnp.where(keep, vv_ref[:n, :], 0.0)
    py = jnp.where(keep, vv_ref[n:, :], 0.0)
    g_ref[...] = combine(3, xy_ref.at[0], xy_ref.at[1], s_ref, px, py, g_ref, work) + unit_rest(n, rank)


def merge_kernel(depth, rank_ref, x_ref, y_ref, mine_ref, theirs_ref, g_ref, s_ref, *work):
    n = g_ref.shape[0]
    rx, ry, rp = rank_at(rank_ref, depth), rank_at(rank_ref, depth, 1), rank_at(rank_ref, depth, 0, 1)
    s_ref[...] = both(n, rx, ry, mine_ref[1] + theirs_ref[1].T)
    px = both(n, rx, rp, mine_ref[0])
    py = both(n, ry, rp, theirs_ref[0])
    g_ref[...] = combine(2, x_ref, y_ref, s_ref, px, py, g_ref, work) + unit_rest(n, rp)


def half_pass(a_ref, keep_ref, reverse, second):
    tiles = a_ref.shape[0] // LANES
    for i in range(tiles // 2, tiles) if second else range(tiles // 2):
        yield from tile_pass(a_ref, keep_ref, reverse, tiles - 1 - i if reverse else i)


def first_kernel(g_ref, half_ref):
    half_ref[...] = g_ref[...]
    together([half_pass(half_ref, None, False, False)])


def middle_kernel(depth, rank_ref, before_ref, g_ref, l_ref, half_ref, a_ref):
    n = g_ref.shape[0]
    a_ref[...] = before_ref[...]
    half_ref[...] = g_ref[...]
    together([half_pass(a_ref, None, False, True), half_pass(half_ref, None, False, False)])
    rank = rank_at(rank_ref, depth - 1)
    l_ref[...] = both(n, rank, rank, a_ref[...])


def factor_of(n, e):
    row, col = iota((n, n), 0), iota((n, n), 1)
    upper = jnp.where(row < col, e, 0.0) + jnp.where(row == col, 1.0 / jnp.where(row == col, e, 1.0), 0.0)
    return upper.T


def group_pair(n, depth, rank_ref):
    pos = lax.axis_index("outer")
    first = jnp.bitwise_and(pos, 1) == 0
    node = jnp.bitwise_and(pos, -2)
    pick = jnp.where(first, 1, 0) + jnp.zeros((n, n), jnp.int32) > 0
    return first, pick, rank_ref[depth, node], rank_ref[depth, node + 1]


def roots_kernel(depth, rank_ref, g_ref, go_ref, c_ref, co_ref, before_ref, *refs):
    n = g_ref.shape[0]
    lower = refs[: depth - 2]
    keep_ref, s_ref, out_ref, l_ref, a_ref, b_ref, h_ref = refs[depth - 2 : depth + 5]
    work = refs[depth + 5 :]
    for i, ref in enumerate(lower):
        out_ref[i] = ref[...]
    first, pick, ra, rb = group_pair(n, depth, rank_ref)
    a_ref[...] = jnp.where(pick, g_ref[...], go_ref[...])
    b_ref[...] = jnp.where(pick, go_ref[...], g_ref[...])
    ca = jnp.where(pick, c_ref[...], co_ref[...])
    cb = jnp.where(pick, co_ref[...], c_ref[...])
    s_ref[...] = both(n, rb, ra, ca.T + cb)
    h_ref[...] = before_ref[...]
    neumann(2, first_power(b_ref, a_ref, s_ref), b_ref, a_ref, s_ref, b_ref[...], l_ref, work)
    turned = thirds(s_ref[...])
    back = dot6(thirds(dot6(turned, thirds(a_ref[...]))), turned, nt=True)
    l_ref[...] = jnp.where(pick, 0.0, back)
    a_ref[...] = jnp.where(pick, a_ref[...], work[0][...])
    together([half_pass(a_ref, keep_ref, True, False), half_pass(h_ref, None, False, True)])
    together([half_pass(a_ref, keep_ref, True, True)])
    rank = rank_at(rank_ref, depth - 1)
    out_ref[depth - 2] = both(n, rank, rank, h_ref[...])
    rank = jnp.where(first, ra, rb)
    out_ref[depth - 1] = both(n, rank, rank, a_ref[...] + l_ref[...])


def top_kernel(depth, rank_ref, k_ref, ko_ref, s_ref, f_ref):
    n = k_ref.shape[0]
    _, pick, _, _ = group_pair(n, depth, rank_ref)
    row, col = iota((n, n), 0), iota((n, n), 1)
    e = jnp.where(pick, k_ref[...], ko_ref[...])
    f_ref[:n, :n] = factor_of(n, e)
    f_ref[:n, n:] = jnp.zeros((n, n), jnp.float32)
    f_ref[n:, :n] = dot6(thirds(s_ref[...]), thirds(jnp.where(row >= col, e, 0.0)), nt=True)
    f_ref[n:, n:] = factor_of(n, jnp.where(pick, ko_ref[...], k_ref[...]))


def call(kernel, outs, n, scratch, *arrays, ranks=None, flops=10**9, held=(), space=pltpu.VMEM, grant=GRANT):
    vmem = pl.BlockSpec(memory_space=pltpu.VMEM)
    lead = [] if ranks is None else [pl.BlockSpec(memory_space=pltpu.SMEM)]
    return pl.pallas_call(
        kernel,
        out_shape=[jax.ShapeDtypeStruct(shape, jnp.float32) for shape in outs],
        in_specs=lead + [pl.BlockSpec(memory_space=space)] * len(arrays),
        out_specs=[vmem] * len(outs),
        scratch_shapes=[*held, *[pltpu.VMEM((n, n), jnp.float32)] * scratch],
        compiler_params=pltpu.CompilerParams(vmem_limit_bytes=grant),
        cost_estimate=pl.CostEstimate(flops=flops, bytes_accessed=4 * 10**6, transcendentals=0),
    )(*([] if ranks is None else [ranks]), *arrays)


def partner(x, axis, bit):
    return lax.ppermute(x, axis, [(i, i ^ 1 << bit) for i in range(lax.axis_size(axis))])


def steps(leaf_blocks, leaf_bases, local_gens, chain_gens, node_ranks):
    n = leaf_bases.shape[2]
    in_levels = chain_gens.shape[0]
    square = (n, n)
    gens = [local_gens[0]]
    others = [partner(gens[0], "inner", 0)]
    pair = pltpu.VMEM((2, n, n), jnp.float32)
    held = (pair, pair, pltpu.VMEM((2 * n, n), jnp.float32), pltpu.SemaphoreType.DMA((4,)))
    arrays = (leaf_blocks[0], leaf_bases[0])
    g = call(leaf_kernel, [square], n, 5, *arrays, ranks=node_ranks, flops=8 * 10**9, held=held, space=pltpu.HBM, grant=WHOLE)[0]
    g_other = partner(g, "inner", 0)
    g, chain_gens = lax.optimization_barrier((g, chain_gens))
    gens = gens + [chain_gens[d] for d in range(in_levels)]
    couple = gens[in_levels][1]
    for d in range(1, in_levels):
        others.append(partner(gens[d], "inner", d))
    other_couple = partner(couple, "outer", 0)
    reduced = []
    half = None
    for depth in range(in_levels):
        if depth == 0:
            half = call(first_kernel, [square], n, 0, g, flops=4 * 10**9)[0]
        else:
            g_other = partner(g, "inner", depth)
            middle = functools.partial(middle_kernel, depth)
            done, half = call(middle, [square] * 2, n, 1, half, g, ranks=node_ranks, flops=4 * 10**9)
            reduced.append(done)
        merge = functools.partial(merge_kernel, depth)
        g = call(merge, [square], n, 5, g, g_other, gens[depth], others[depth], ranks=node_ranks)[0]
    g_other = partner(g, "outer", 0)
    roots = functools.partial(roots_kernel, in_levels)
    arrays = (g, g_other, couple, other_couple, half, *reduced[1:])
    outs = [square, square, (in_levels, n, n)]
    e, s, chain = call(roots, outs, n, 8, *arrays, ranks=node_ranks, flops=4 * 10**9)
    e_other = partner(e, "outer", 0)
    top = functools.partial(top_kernel, in_levels)
    factor = call(top, [(2 * n, 2 * n)], n, 0, e, e_other, s, ranks=node_ranks, flops=4 * 10**9)[0]
    return (reduced[0][None], chain, factor)


def solution(mesh):
    return jax.shard_map(
        steps,
        mesh=mesh,
        in_specs=(
            P(("outer", "inner"), None, None),
            P(("outer", "inner"), None, None),
            P(("outer", "inner"), None, None, None),
            P(("outer", "inner"), None, None, None),
            P(),
        ),
        out_specs=(
            P(("outer", "inner"), None, None),
            P(("outer", "inner"), None, None),
            P(("outer", "inner"), None),
        ),
        check_vma=False,
    )
```
